512 devices in a mesh: row: 16 (over z_hi, y), col: 32 (over z_lo, x, core).
Axes of the slice: x: 4, y: 4, z: 16 (z_hi: 4, z_lo: 4; z = z_hi * 4 + z_lo), core: 2. Of those that a mesh axis runs over, the one named last changes fastest.
Arguments:
- grad_out: bfloat16 [65536, 512], P(('row', 'col'))
- relu_mask: int32 [65536, 512], P(('row', 'col')), may hold values 0 or 1
- aggregated: bfloat16 [65536, 512], P(('row', 'col')), may hold values from -6 to 6
- weight: bfloat16 [512, 512], replicated, may hold values from -0.25 to 0.25
- adj_blocks: bfloat16 [16, 32, 85, 128, 128], P('row', 'col'), may hold values from 0 to 0.02876383
- block_pos: int32 [16, 32, 85], P('row', 'col'), may hold values from 0 to 511, as said below
- block_live: int32 [16, 32], P('row', 'col'), may hold values from 1 to 85, as said below
Outputs:
- grad_input: bfloat16 [32, 2048, 512], P('col', 'row')
- grad_weight: float32 [512, 512], replicated
- grad_bias: float32 [512], replicated
The draws below stay inside these ranges and needn't reach their ends.
Inputs may be any that keep to these rules, and one draw needn't show every extreme that they name: `block_pos`: within one tile the 85 slots name different positions; position p is block row p // 16, block column p % 16. `block_live`: some tile uses all 85 slots.
All inputs are finite; a program needn't handle non-finite values. No bound on the sum of `relu_mask` on one device may be relied on, other than what follows from the above.
Results may differ from the reference program's by a relative error of at most 0.005.
Values may be sent and summed in bfloat16 or wider, within the bound.
No kernel may reach another device: no remote copies, remote signals or barrier semaphores. Data moves between devices by JAX's collectives and lax.ppermute only.
A program may use at most 64 MiB of HBM per device.

```python
import math
import jax
import jax.numpy as jnp
from jax import lax

FEAT = 512
BLK = 128
NODES = 65536
TBR = 32
TBC = 16
CAP = 85
N_ROW = 16
N_COL = 32


def draw_grad_out(key, part):
    first_key, second_key = jax.random.split(key, 2)
    order = jnp.arange(NODES, dtype=jnp.float32)
    rising = 1.0 + 2.0 * order / max(NODES - 1, 1)
    rough = jnp.exp(jax.random.uniform(second_key, (NODES,), jnp.float32, math.log(0.15), math.log(1.5)))
    values = jax.random.normal(first_key, (NODES, FEAT), jnp.float32)
    return (values * (rising * rough)[:, None]).astype(jnp.bfloat16)


def draw_adj_blocks(key, part):
    first_key = jax.random.fold_in(jax.random.fold_in(key, 7), 0)
    fan_in = BLK * CAP * N_ROW // (3 * TBC)
    top = math.sqrt(3.0 / fan_in) * 0.99
    shape = (N_ROW, N_COL, CAP, BLK, BLK)
    values = jax.random.uniform(first_key, shape, jnp.float32, 0.0, 1.0) * top
    return values.astype(jnp.bfloat16)


def draw_block_pos(key, part):
    position_count = TBR * TBC
    tile_keys = jax.random.split(key, N_ROW * N_COL)
    chosen = jax.vmap(lambda item: jax.random.permutation(item, position_count)[:CAP])(tile_keys).astype(jnp.int32)
    holder = jnp.any(chosen[0] == position_count - 1)
    first_tile = jnp.where(holder, chosen[0], chosen[0].at[0].set(position_count - 1))
    chosen = chosen.at[0].set(first_tile)
    return chosen.reshape(N_ROW, N_COL, CAP)


def draw_block_live(key, part):
    first_key, second_key = jax.random.split(key)
    sampled = jax.random.randint(first_key, (N_ROW * N_COL,), 1, CAP + 1)
    counts = jnp.maximum(1, sampled * sampled // CAP)
    fullest = jax.random.randint(second_key, (), 0, N_ROW * N_COL)
    counts = jnp.where(jnp.arange(N_ROW * N_COL) == fullest, CAP, counts)
    return counts.astype(jnp.int32).reshape(N_ROW, N_COL)


def set_ends(entries, rng, low, largest):
    longest = entries.shape.index(max(entries.shape))
    spots = []
    for shift in (0, 1):
        where = [jax.random.randint(jax.random.fold_in(rng, axis), (), 0, length) for axis, length in enumerate(entries.shape)]
        where[longest] = (where[longest] + shift) % entries.shape[longest]
        spots.append(tuple(where))
    return entries.at[spots[0]].set(low).at[spots[1]].set(largest)


def shard_levels(rng, dims, cuts, least, largest):
    def one(dim, parts):
        draws = jax.random.uniform(jax.random.fold_in(jax.random.fold_in(rng, 6), dim), (parts,), jnp.float32, least / len(cuts), largest / len(cuts))
        return jnp.repeat(jnp.exp(draws), dims[dim] // parts).reshape((-1,) + (1,) * (len(dims) - dim - 1))

    factor_of = one(*cuts[0])
    for cut in cuts[1:]:
        factor_of = factor_of * one(*cut)
    return factor_of


def scatter_about(stream_key, dims, deviation, reach, shards=(), kind=jnp.bfloat16):
    level = shard_levels(stream_key, dims, shards, -0.22, 0.18) if shards else 1.0
    entries = jax.random.normal(stream_key, dims, jnp.float32) * deviation * level
    return jnp.minimum(jnp.maximum(entries, -reach), reach).astype(kind)


def setup_inputs(seed: int = 0) -> dict:
    key_list = jax.random.split(jax.random.key(seed), 8)
    return {
        "grad_out": draw_grad_out(jax.random.fold_in(key_list[7], 71), 0),
        "relu_mask": set_ends((jax.random.randint(key_list[1], (NODES, FEAT), 0, 2) < 1).astype(jnp.int32), jax.random.fold_in(key_list[1], 1), 0, 1),
        "aggregated": scatter_about(key_list[2], (NODES, FEAT), 1.0, 6.0, ((0, 512),)),
        "weight": scatter_about(key_list[3], (FEAT, FEAT), FEAT ** -0.5, 0.25),
        "adj_blocks": draw_adj_blocks(jax.random.fold_in(key_list[7], 71), 0),
        "block_pos": draw_block_pos(jax.random.fold_in(key_list[7], 71), 0),
        "block_live": draw_block_live(jax.random.fold_in(key_list[7], 71), 0),
    }


def reference(grad_out, relu_mask, aggregated, weight, adj_blocks, block_pos, block_live):
    grad_pre = grad_out * relu_mask.astype(jnp.bfloat16)
    gradient_row_slice = jnp.dot(grad_pre, weight.T, preferred_element_type=jnp.float32).astype(jnp.bfloat16)
    tile_height = NODES // N_ROW

    def one_column(tile_col):

        def add_tile(running_total, tile_row):
            stacked_tiles = lax.dynamic_slice_in_dim(gradient_row_slice, tile_row * tile_height, tile_height, 0)
            stacked_tiles = stacked_tiles.reshape(TBR, BLK, FEAT).astype(jnp.float32)
            positions = block_pos[tile_row, tile_col]
            blocks = adj_blocks[tile_row, tile_col].astype(jnp.float32)
            picked = stacked_tiles[positions // TBC]
            alive = (jnp.arange(CAP, dtype=jnp.int32) < block_live[tile_row, tile_col]).astype(jnp.float32)
            partial_products = jnp.einsum('kab,kaf->kbf', blocks, picked) * alive[:, None, None]
            insert_position = ((positions % TBC)[:, None] == jnp.arange(TBC, dtype=jnp.int32)[None, :]).astype(jnp.float32)
            return (running_total + jnp.einsum('lj,lsu->jsu', insert_position, partial_products), None)
        start_sum = jnp.zeros((TBC, BLK, FEAT), jnp.float32)
        running_total, _ = lax.scan(add_tile, start_sum, jnp.arange(N_ROW, dtype=jnp.int32))
        return running_total.reshape(TBC * BLK, FEAT)
    full_input = lax.map(one_column, jnp.arange(N_COL, dtype=jnp.int32))
    grad_input = full_input.astype(jnp.bfloat16)
    factor = 1.0 / math.sqrt(NODES)
    grad_weight = jnp.einsum('nf,ng->fg', aggregated.astype(jnp.float32), grad_pre.astype(jnp.float32)) * factor
    grad_bias = lax.optimization_barrier(jnp.sum(grad_pre.astype(jnp.float32), axis=0)) * factor
    return (grad_input, grad_weight, grad_bias)
```

```python
import math

import jax
import jax.numpy as jnp
from jax import lax
from jax.experimental import pallas as pl
from jax.experimental.pallas import tpu as pltpu
from jax.sharding import Mesh, PartitionSpec as P

F32 = jnp.float32
BF16 = jnp.bfloat16
VMEM_LIMIT = 48 * 1024 * 1024


def split_terms(value):
    high = value.astype(BF16)
    low = (value - high.astype(F32)).astype(BF16)
    return high, low


def tile_kernel(pos_ref, live_ref, core_ref, blocks_ref, own_ref, other_ref, out_ref, acc_ref):
    n_zh = 4
    blk = blocks_ref.shape[-1]
    n_x = own_ref.shape[0]
    gathered = out_ref.shape[0]
    n_feat = own_ref.shape[-1]
    tile_cols = acc_ref.shape[0]
    n_rows = own_ref.shape[1] - (out_ref.shape[1] - n_zh * blk - 16) // 2
    acc_ref[...] = jnp.zeros_like(acc_ref)
    my_core = core_ref[0]

    def add_block(slot, carry):
        position = pos_ref[slot]
        source = position // tile_cols
        column = position % tile_cols
        z_part = source // (2 * n_x)
        x_part = (source // 2) % n_x
        mine = source % 2 == my_core
        first = pl.multiple_of(z_part * blk, blk)
        rows = jnp.where(mine, own_ref[x_part, pl.ds(first, blk), :], other_ref[x_part, pl.ds(first, blk), :])
        acc_ref[column] += lax.dot_general(
            blocks_ref[slot], rows, (((0,), (0,)), ((), ())), preferred_element_type=F32
        )
        return carry

    lax.fori_loop(0, live_ref[0], add_block, 0)

    n_slice = own_ref.shape[1] - n_rows
    weight_terms = jnp.zeros((n_slice, n_feat), F32)
    bias_terms = jnp.zeros((8, n_feat), F32)
    ones = jnp.ones((8, n_rows), BF16)
    for ref in (own_ref, other_ref):
        for x in range(n_x):
            rows = ref[x, :n_rows, :]
            weight_terms += jnp.dot(ref[x, n_rows:, :], rows, preferred_element_type=F32)
            bias_terms += jnp.dot(ones, rows, preferred_element_type=F32)
    terms = jnp.concatenate([weight_terms, bias_terms], axis=0)
    high, low = split_terms(terms)
    both = jnp.concatenate([high, low], axis=0)
    for y in range(gathered):
        for z in range(n_zh):
            out_ref[y, z * blk : (z + 1) * blk, :] = acc_ref[z * gathered + y].astype(BF16)
        out_ref[y, n_zh * blk :, :] = both


def fold_kernel(in_ref, out_ref):
    n_src = in_ref.shape[0]
    n_dst, width, _ = out_ref.shape
    n_terms = (in_ref.shape[1] - n_dst * (width - (in_ref.shape[1] - n_dst * 128))) // 2
    blk = width - 2 * n_terms
    for z in range(n_dst):
        total = in_ref[0, z * blk : (z + 1) * blk, :].astype(F32)
        for s in range(1, n_src):
            total += in_ref[s, z * blk : (z + 1) * blk, :].astype(F32)
        out_ref[z, :blk, :] = total.astype(BF16)
    base = n_dst * blk
    terms = jnp.zeros((n_terms, in_ref.shape[2]), F32)
    for s in range(n_src):
        terms += in_ref[s, base : base + n_terms, :].astype(F32) + in_ref[s, base + n_terms :, :].astype(F32)
    high, low = split_terms(terms)
    both = jnp.concatenate([high, low], axis=0)
    for z in range(n_dst):
        out_ref[z, blk:, :] = both


def last_kernel(in_ref, weight_ref, rows_ref, grad_ref, bias_ref, *, factor):
    n_src, width, _ = in_ref.shape
    blk = rows_ref.shape[0]
    n_terms = (width - blk) // 2
    total = in_ref[0, :blk, :].astype(F32)
    for s in range(1, n_src):
        total += in_ref[s, :blk, :].astype(F32)
    high, low = split_terms(total)
    dims = (((1,), (1,)), ((), ()))
    product = lax.dot_general(high, weight_ref[...], dims, preferred_element_type=F32)
    product += lax.dot_general(low, weight_ref[...], dims, preferred_element_type=F32)
    rows_ref[...] = product.astype(BF16)
    terms = jnp.zeros((n_terms, in_ref.shape[2]), F32)
    for s in range(n_src):
        terms += in_ref[s, blk : blk + n_terms, :].astype(F32) + in_ref[s, blk + n_terms :, :].astype(F32)
    terms = terms * factor
    n_slice = n_terms - 8
    slice_rows = terms[:n_slice].astype(BF16)
    for z in range(grad_ref.shape[0]):
        grad_ref[z] = slice_rows
    bias_ref[...] = terms[n_slice:]


def call(kernel, out_shape, scratch=(), n_scalar=0, n_in=1):
    smem = pl.BlockSpec(memory_space=pltpu.SMEM)
    vmem = pl.BlockSpec(memory_space=pltpu.VMEM)
    return pl.pallas_call(
        kernel,
        out_shape=out_shape,
        in_specs=[smem] * n_scalar + [vmem] * n_in,
        out_specs=jax.tree.map(lambda _: vmem, out_shape),
        scratch_shapes=list(scratch),
        compiler_params=pltpu.CompilerParams(vmem_limit_bytes=VMEM_LIMIT),
    )


def swap(value, axis):
    return lax.all_to_all(value, axis, split_axis=0, concat_axis=0, tiled=True)


def body(grad_out, relu_mask, aggregated, weight, adj_blocks, block_pos, block_live):
    blk, n_feat = grad_out.shape
    n_zh, n_y, n_zl, n_x, n_core = (lax.axis_size(a) for a in ("zh", "y", "zl", "x", "core"))
    n_rows = n_zl * blk
    n_slice = n_feat // (n_zl * n_x)
    n_terms = n_slice + 8
    grad_pre = grad_out * relu_mask.astype(BF16)
    columns = aggregated.T.reshape(n_zl, n_x, n_slice, blk).transpose(0, 2, 1, 3)
    columns = columns.reshape(n_zl, n_slice, n_x * blk)
    sent = jnp.concatenate([jnp.broadcast_to(grad_pre, (n_zl, blk, n_feat)), columns], axis=1)
    got = swap(sent, "zl")
    rows = got[:, :blk].reshape(n_rows, n_feat)
    columns = got[:, blk:].reshape(n_zl, n_slice, n_x, blk).transpose(2, 1, 0, 3)
    columns = columns.reshape(n_x, n_slice, n_rows)
    sent = jnp.concatenate([jnp.broadcast_to(rows, (n_x, n_rows, n_feat)), columns], axis=1)
    own = swap(sent, "x")
    other = lax.ppermute(own, "core", [(0, 1), (1, 0)])
    sent = call(
        tile_kernel,
        jax.ShapeDtypeStruct((n_y, n_zh * blk + 2 * n_terms, n_feat), BF16),
        scratch=[pltpu.VMEM((n_zh * n_y, blk, n_feat), F32)],
        n_scalar=3,
        n_in=3,
    )(
        block_pos.reshape(-1),
        block_live.reshape(-1),
        lax.axis_index("core").astype(jnp.int32).reshape(1),
        adj_blocks[0, 0],
        own,
        other,
    )
    got = swap(sent, "y")
    sent = call(fold_kernel, jax.ShapeDtypeStruct((n_zh, blk + 2 * n_terms, n_feat), BF16))(got)
    got = swap(sent, "zh")
    factor = 1.0 / math.sqrt(blk * n_zh * n_y * n_zl * n_x * n_core)

    def last(in_ref, weight_ref, rows_ref, grad_ref, bias_ref):
        last_kernel(in_ref, weight_ref, rows_ref, grad_ref, bias_ref, factor=factor)

    out_rows, part, bias = call(
        last,
        (
            jax.ShapeDtypeStruct((blk, n_feat), BF16),
            jax.ShapeDtypeStruct((n_zl, n_slice, n_feat), BF16),
            jax.ShapeDtypeStruct((8, n_feat), F32),
        ),
        n_in=2,
    )(got, weight)
    part = swap(part, "zl").reshape(n_rows // blk * n_slice, n_feat)
    part = swap(jnp.broadcast_to(part, (n_x,) + part.shape), "x")
    part = part.reshape(n_x, n_zl, n_slice, n_feat).transpose(1, 0, 2, 3)
    return out_rows[None], part.reshape(n_feat, n_feat).astype(F32), bias[0]


def solution(mesh):
    fine = Mesh(mesh.devices.reshape(4, 4, 4, 4, 2), ("zh", "y", "zl", "x", "core"))
    row, col = ("zh", "y"), ("zl", "x", "core")
    return jax.shard_map(
        body,
        mesh=fine,
        in_specs=(
            P(row + col, None),
            P(row + col, None),
            P(row + col, None),
            P(),
            P(row, col, None, None, None),
            P(row, col, None),
            P(row, col),
        ),
        out_specs=(P(col, row, None), P(), P()),
        check_vma=False,
    )
```

```python
import functools
import math

import jax
import jax.numpy as jnp
from jax import lax
from jax.experimental import pallas as pl
from jax.experimental.pallas import tpu as pltpu
from jax.sharding import Mesh, PartitionSpec as P

F32 = jnp.float32
BF16 = jnp.bfloat16
VMEM_LIMIT = 48 * 1024 * 1024


def tile_kernel(pos_ref, live_ref, core_ref, blocks_ref, own_ref, other_ref, out_ref, acc_ref, *, group, n_x):
    n_y, width, _ = out_ref.shape
    blk = blocks_ref.shape[-1]
    tile_cols = acc_ref.shape[0]
    acc_ref[...] = jnp.zeros_like(acc_ref)
    my_core = core_ref[0]
    live = live_ref[0]

    def add_group(turn, carry):
        found = []
        for k in range(group):
            slot = turn * group + k
            position = pos_ref[slot]
            source = position // tile_cols
            first = pl.multiple_of(source // (2 * n_x) * blk, blk)
            x_part = (source // 2) % n_x
            rows = jnp.where(
                source % 2 == my_core, own_ref[x_part, pl.ds(first, blk), :], other_ref[x_part, pl.ds(first, blk), :]
            )
            block = blocks_ref[slot]
            block = jnp.where(slot < live, block, jnp.zeros_like(block))
            product = lax.dot_general(block, rows, (((0,), (0,)), ((), ())), preferred_element_type=F32)
            found.append((position % tile_cols, product))
        for column, product in found:
            acc_ref[column] += product
        return carry

    lax.fori_loop(0, (live + group - 1) // group, add_group, 0)
    for y in range(n_y):
        for z in range(width // blk):
            out_ref[y, z * blk : (z + 1) * blk, :] = acc_ref[z * n_y + y].astype(BF16)


def terms_kernel(core_ref, own_ref, other_ref, out_ref, *, n_rows):
    n_x, _, n_feat = own_ref.shape
    n_slice = out_ref.shape[1] - 8
    first = pl.multiple_of(n_rows + core_ref[0] * n_slice, n_slice)
    weight_terms = jnp.zeros((n_slice, n_feat), F32)
    bias_terms = jnp.zeros((8, n_feat), F32)
    ones = jnp.ones((8, n_rows), BF16)
    for ref in (own_ref, other_ref):
        for x in range(n_x):
            rows = ref[x, :n_rows, :]
            weight_terms += jnp.dot(ref[x, pl.ds(first, n_slice), :], rows, preferred_element_type=F32)
            bias_terms += jnp.dot(ones, rows, preferred_element_type=F32)
    for y in range(out_ref.shape[0]):
        out_ref[y, :n_slice, :] = weight_terms
        out_ref[y, n_slice:, :] = bias_terms


def fold_kernel(in_ref, out_ref):
    total = in_ref[0].astype(F32)
    for s in range(1, in_ref.shape[0]):
        total += in_ref[s].astype(F32)
    out_ref[...] = total.astype(BF16)


def fold_terms_kernel(in_ref, out_ref):
    total = in_ref[0]
    for s in range(1, in_ref.shape[0]):
        total += in_ref[s]
    for z in range(out_ref.shape[0]):
        out_ref[z] = total


def last_kernel(in_ref, weight_ref, rows_ref):
    total = in_ref[0].astype(F32)
    for s in range(1, in_ref.shape[0]):
        total += in_ref[s].astype(F32)
    high = total.astype(BF16)
    low = (total - high.astype(F32)).astype(BF16)
    dims = (((1,), (1,)), ((), ()))
    product = lax.dot_general(high, weight_ref[...], dims, preferred_element_type=F32)
    product += lax.dot_general(low, weight_ref[...], dims, preferred_element_type=F32)
    rows_ref[...] = product.astype(BF16)


def call(kernel, out_shape, scratch=(), n_scalar=0, n_in=1):
    smem = pl.BlockSpec(memory_space=pltpu.SMEM)
    vmem = pl.BlockSpec(memory_space=pltpu.VMEM)
    return pl.pallas_call(
        kernel,
        out_shape=out_shape,
        in_specs=[smem] * n_scalar + [vmem] * n_in,
        out_specs=jax.tree.map(lambda _: vmem, out_shape),
        scratch_shapes=list(scratch),
        compiler_params=pltpu.CompilerParams(vmem_limit_bytes=VMEM_LIMIT),
    )


def swap(value, axis):
    return lax.all_to_all(value, axis, split_axis=0, concat_axis=0, tiled=True)


def body(grad_out, relu_mask, aggregated, weight, adj_blocks, block_pos, block_live):
    blk, n_feat = grad_out.shape
    n_zh, n_y, n_zl, n_x, n_core = (lax.axis_size(a) for a in ("zh", "y", "zl", "x", "core"))
    n_rows = n_zl * blk
    n_pair = n_feat // (n_zl * n_x)
    n_slice = n_pair // n_core
    n_terms = n_slice + 8
    grad_pre = grad_out * relu_mask.astype(BF16)
    columns = aggregated.T.reshape(n_zl, n_x, n_pair, blk).transpose(0, 2, 1, 3)
    columns = columns.reshape(n_zl, n_pair, n_x * blk)
    sent = jnp.concatenate([jnp.broadcast_to(grad_pre, (n_zl, blk, n_feat)), columns], axis=1)
    got = swap(sent, "zl")
    rows = got[:, :blk].reshape(n_rows, n_feat)
    columns = got[:, blk:].reshape(n_zl, n_pair, n_x, blk).transpose(2, 1, 0, 3)
    columns = columns.reshape(n_x, n_pair, n_rows)
    sent = jnp.concatenate([jnp.broadcast_to(rows, (n_x, n_rows, n_feat)), columns], axis=1)
    own = swap(sent, "x")
    other = lax.ppermute(own, "core", [(0, 1), (1, 0)])
    core = lax.axis_index("core").astype(jnp.int32).reshape(1)
    terms = call(
        functools.partial(terms_kernel, n_rows=n_rows),
        jax.ShapeDtypeStruct((n_y, n_terms, n_feat), F32),
        n_scalar=1,
        n_in=2,
    )(core, own, other)
    terms = swap(terms, "y")
    slots = adj_blocks.shape[2]
    group = max(d for d in range(1, 9) if slots % d == 0)
    sent = call(
        functools.partial(tile_kernel, group=group, n_x=n_x),
        jax.ShapeDtypeStruct((n_y, n_zh * blk, n_feat), BF16),
        scratch=[pltpu.VMEM((n_zh * n_y, blk, n_feat), F32)],
        n_scalar=3,
        n_in=3,
    )(block_pos.reshape(-1), block_live.reshape(-1), core, adj_blocks[0, 0], own, other)
    terms, sent = lax.optimization_barrier((terms, sent))
    terms = call(fold_terms_kernel, jax.ShapeDtypeStruct((n_zh, n_terms, n_feat), F32))(terms)
    terms = swap(terms, "zh").sum(axis=0)
    factor = 1.0 / math.sqrt(blk * n_zh * n_y * n_zl * n_x * n_core)
    terms = terms * factor
    terms, sent = lax.optimization_barrier((terms, sent))
    grad_weight = lax.all_gather(terms[:n_slice], ("zl", "x", "core"), axis=0, tiled=True)
    got = swap(sent, "y")
    sent = call(fold_kernel, jax.ShapeDtypeStruct((n_zh * blk, n_feat), BF16))(got)
    got = swap(sent.reshape(n_zh, blk, n_feat), "zh")
    out_rows = call(last_kernel, jax.ShapeDtypeStruct((blk, n_feat), BF16), n_in=2)(got, weight)
    return out_rows[None], grad_weight, terms[n_slice]


def solution(mesh):
    fine = Mesh(mesh.devices.reshape(4, 4, 4, 4, 2), ("zh", "y", "zl", "x", "core"))
    row, col = ("zh", "y"), ("zl", "x", "core")
    return jax.shard_map(
        body,
        mesh=fine,
        in_specs=(
            P(row + col, None),
            P(row + col, None),
            P(row + col, None),
            P(),
            P(row, col, None, None, None),
            P(row, col, None),
            P(row, col),
        ),
        out_specs=(P(col, row, None), P(), P()),
        check_vma=False,
    )
```

```python
import functools
import math

import jax
import jax.numpy as jnp
from jax import lax
from jax.experimental import pallas as pl
from jax.experimental.pallas import tpu as pltpu
from jax.sharding import Mesh, PartitionSpec as P

F32 = jnp.float32
BF16 = jnp.bfloat16
VMEM_LIMIT = 48 * 1024 * 1024


def tile_kernel(pos_ref, live_ref, core_ref, blocks_ref, own_ref, other_ref, out_ref, acc_ref, *, group, n_x):
    n_y, width, _ = out_ref.shape
    blk = blocks_ref.shape[-1]
    tile_cols = acc_ref.shape[0]
    acc_ref[...] = jnp.zeros_like(acc_ref)
    my_core = core_ref[0]
    live = live_ref[0]

    def add_group(turn, carry):
        found = []
        for k in range(group):
            slot = turn * group + k
            position = pos_ref[slot]
            source = position // tile_cols
            first = pl.multiple_of(source // (2 * n_x) * blk, blk)
            x_part = (source // 2) % n_x
            rows = jnp.where(
                source % 2 == my_core, own_ref[x_part, pl.ds(first, blk), :], other_ref[x_part, pl.ds(first, blk), :]
            )
            block = blocks_ref[slot]
            block = jnp.where(slot < live, block, jnp.zeros_like(block))
            product = lax.dot_general(block, rows, (((0,), (0,)), ((), ())), preferred_element_type=F32)
            found.append((position % tile_cols, product))
        for column, product in found:
            acc_ref[column] += product
        return carry

    lax.fori_loop(0, (live + group - 1) // group, add_group, 0)
    for y in range(n_y):
        for z in range(width // blk):
            out_ref[y, z * blk : (z + 1) * blk, :] = acc_ref[z * n_y + y].astype(BF16)


def terms_kernel(core_ref, own_ref, other_ref, out_ref, *, n_rows):
    n_x, _, n_feat = own_ref.shape
    n_slice = out_ref.shape[0] - 8
    first = pl.multiple_of(n_rows + core_ref[0] * n_slice, n_slice)
    weight_terms = jnp.zeros((n_slice, n_feat), F32)
    bias_terms = jnp.zeros((8, n_feat), F32)
    ones = jnp.ones((8, n_rows), BF16)
    for ref in (own_ref, other_ref):
        for x in range(n_x):
            rows = ref[x, :n_rows, :]
            weight_terms += jnp.dot(ref[x, pl.ds(first, n_slice), :], rows, preferred_element_type=F32)
            bias_terms += jnp.dot(ones, rows, preferred_element_type=F32)
    out_ref[:n_slice, :] = weight_terms
    out_ref[n_slice:, :] = bias_terms


def fold_kernel(in_ref, out_ref):
    total = in_ref[0].astype(F32)
    for s in range(1, in_ref.shape[0]):
        total += in_ref[s].astype(F32)
    out_ref[...] = total.astype(BF16)


def place_kernel(index_ref, *refs):
    out_ref = refs[-1]
    n_slice = refs[0].shape[0]
    offset = 0
    for ref in refs[:-1]:
        for k in range(ref.shape[0] // n_slice):
            first = pl.multiple_of((index_ref[0] ^ index_ref[1 + offset]) * n_slice, n_slice)
            out_ref[pl.ds(first, n_slice), :] = ref[k * n_slice : (k + 1) * n_slice, :]
            offset += 1


def last_kernel(in_ref, weight_ref, rows_ref):
    total = in_ref[0].astype(F32)
    for s in range(1, in_ref.shape[0]):
        total += in_ref[s].astype(F32)
    high = total.astype(BF16)
    low = (total - high.astype(F32)).astype(BF16)
    dims = (((1,), (1,)), ((), ()))
    product = lax.dot_general(high, weight_ref[...], dims, preferred_element_type=F32)
    product += lax.dot_general(low, weight_ref[...], dims, preferred_element_type=F32)
    rows_ref[...] = product.astype(BF16)


def call(kernel, out_shape, scratch=(), n_scalar=0, n_in=1):
    smem = pl.BlockSpec(memory_space=pltpu.SMEM)
    vmem = pl.BlockSpec(memory_space=pltpu.VMEM)
    return pl.pallas_call(
        kernel,
        out_shape=out_shape,
        in_specs=[smem] * n_scalar + [vmem] * n_in,
        out_specs=jax.tree.map(lambda _: vmem, out_shape),
        scratch_shapes=list(scratch),
        compiler_params=pltpu.CompilerParams(vmem_limit_bytes=VMEM_LIMIT),
    )


def swap(value, axis):
    return lax.all_to_all(value, axis, split_axis=0, concat_axis=0, tiled=True)


def trade(value, axis, bit):
    return lax.ppermute(value, axis, [(i, i ^ bit) for i in range(lax.axis_size(axis))])


def body(grad_out, relu_mask, aggregated, weight, adj_blocks, block_pos, block_live):
    blk, n_feat = grad_out.shape
    n_zh, n_y, n_zl, n_x, n_core = (lax.axis_size(a) for a in ("zh", "y", "zl", "x", "core"))
    n_rows = n_zl * blk
    n_pair = n_feat // (n_zl * n_x)
    n_slice = n_pair // n_core
    n_terms = n_slice + 8
    grad_pre = grad_out * relu_mask.astype(BF16)
    columns = aggregated.T.reshape(n_zl, n_x, n_pair, blk).transpose(0, 2, 1, 3)
    columns = columns.reshape(n_zl, n_pair, n_x * blk)
    sent = jnp.concatenate([jnp.broadcast_to(grad_pre, (n_zl, blk, n_feat)), columns], axis=1)
    got = swap(sent, "zl")
    rows = got[:, :blk].reshape(n_rows, n_feat)
    columns = got[:, blk:].reshape(n_zl, n_pair, n_x, blk).transpose(2, 1, 0, 3)
    columns = columns.reshape(n_x, n_pair, n_rows)
    sent = jnp.concatenate([jnp.broadcast_to(rows, (n_x, n_rows, n_feat)), columns], axis=1)
    own = swap(sent, "x")
    other = lax.ppermute(own, "core", [(0, 1), (1, 0)])
    core = lax.axis_index("core").astype(jnp.int32).reshape(1)
    slots = adj_blocks.shape[2]
    group = max(d for d in range(1, 9) if slots % d == 0)
    sent = call(
        functools.partial(tile_kernel, group=group, n_x=n_x),
        jax.ShapeDtypeStruct((n_y, n_zh * blk, n_feat), BF16),
        scratch=[pltpu.VMEM((n_zh * n_y, blk, n_feat), F32)],
        n_scalar=3,
        n_in=3,
    )(block_pos.reshape(-1), block_live.reshape(-1), core, adj_blocks[0, 0], own, other)
    own, other, sent = lax.optimization_barrier((own, other, sent))
    terms = call(
        functools.partial(terms_kernel, n_rows=n_rows),
        jax.ShapeDtypeStruct((n_terms, n_feat), F32),
        n_scalar=1,
        n_in=2,
    )(core, own, other)
    for axis in ("y", "zh"):
        for bit in (1, 2):
            terms = terms + trade(terms, axis, bit)
    factor = 1.0 / math.sqrt(blk * n_zh * n_y * n_zl * n_x * n_core)
    terms = terms * factor
    pieces = [terms[:n_slice]]
    offsets = [0]
    for axis, bit, stride in (
        ("zl", 1, n_x * n_core),
        ("zl", 2, n_x * n_core),
        ("x", 1, n_core),
        ("x", 2, n_core),
        ("core", 1, 1),
    ):
        pieces.append(trade(jnp.concatenate(pieces, axis=0), axis, bit))
        offsets += [o ^ (bit * stride) for o in offsets]
    place = lax.axis_index(("zl", "x", "core")).astype(jnp.int32)
    grad_weight = call(place_kernel, jax.ShapeDtypeStruct((n_feat, n_feat), F32), n_scalar=1, n_in=len(pieces))(
        jnp.concatenate([place.reshape(1), jnp.array(offsets, jnp.int32)]), *pieces
    )
    got = swap(sent, "y")
    sent = call(fold_kernel, jax.ShapeDtypeStruct((n_zh * blk, n_feat), BF16))(got)
    got = swap(sent.reshape(n_zh, blk, n_feat), "zh")
    out_rows = call(last_kernel, jax.ShapeDtypeStruct((blk, n_feat), BF16), n_in=2)(got, weight)
    return out_rows[None], grad_weight, terms[n_slice]


def solution(mesh):
    fine = Mesh(mesh.devices.reshape(4, 4, 4, 4, 2), ("zh", "y", "zl", "x", "core"))
    row, col = ("zh", "y"), ("zl", "x", "core")
    return jax.shard_map(
        body,
        mesh=fine,
        in_specs=(
            P(row + col, None),
            P(row + col, None),
            P(row + col, None),
            P(),
            P(row, col, None, None, None),
            P(row, col, None),
            P(row, col),
        ),
        out_specs=(P(col, row, None), P(), P()),
        check_vma=False,
    )
```

```python
import functools
import math

import jax
import jax.numpy as jnp
from jax import lax
from jax.experimental import pallas as pl
from jax.experimental.pallas import tpu as pltpu
from jax.sharding import Mesh, PartitionSpec as P

F32 = jnp.float32
BF16 = jnp.bfloat16
MARK = jax.ShapeDtypeStruct((8, 128), F32)
VMEM_LIMIT = 48 * 1024 * 1024


def tile_kernel(pos_ref, live_ref, core_ref, blocks_ref, own_ref, other_ref, out_ref, mark_ref, acc_ref, low_ref, sems, *, group, n_x):
    n_y, width, _ = out_ref.shape
    blk = blocks_ref.shape[-1]
    tile_cols = acc_ref.shape[0]
    acc_ref[...] = jnp.zeros_like(acc_ref)
    my_core = core_ref[0]
    live = live_ref[0]

    def add_group(turn, carry):
        found = []
        for k in range(group):
            slot = turn * group + k
            position = pos_ref[slot]
            source = position // tile_cols
            first = pl.multiple_of(source // (2 * n_x) * blk, blk)
            x_part = (source // 2) % n_x
            rows = jnp.where(
                source % 2 == my_core, own_ref[x_part, pl.ds(first, blk), :], other_ref[x_part, pl.ds(first, blk), :]
            )
            block = blocks_ref[slot]
            block = jnp.where(slot < live, block, jnp.zeros_like(block))
            product = lax.dot_general(block, rows, (((0,), (0,)), ((), ())), preferred_element_type=F32)
            found.append((position % tile_cols, product))
        for column, product in found:
            acc_ref[column] += product
        return carry

    lax.fori_loop(0, (live + group - 1) // group, add_group, 0)
    copies = []
    for y in range(n_y):
        for z in range(width // blk):
            low_ref[y, z * blk : (z + 1) * blk, :] = acc_ref[z * n_y + y].astype(BF16)
        copies.append(pltpu.make_async_copy(low_ref.at[y], out_ref.at[y], sems.at[y]))
        copies[-1].start()
    mark_ref[...] = jnp.zeros_like(mark_ref)
    for copy in copies:
        copy.wait()


def terms_kernel(core_ref, own_ref, other_ref, out_ref, *, n_rows):
    n_x, _, n_feat = own_ref.shape
    n_slice = out_ref.shape[0] - 8
    first = pl.multiple_of(n_rows + core_ref[0] * n_slice, n_slice)
    weight_terms = jnp.zeros((n_slice, n_feat), F32)
    bias_terms = jnp.zeros((8, n_feat), F32)
    ones = jnp.ones((8, n_rows), BF16)
    for ref in (own_ref, other_ref):
        for x in range(n_x):
            rows = ref[x, :n_rows, :]
            weight_terms += jnp.dot(ref[x, pl.ds(first, n_slice), :], rows, preferred_element_type=F32)
            bias_terms += jnp.dot(ones, rows, preferred_element_type=F32)
    out_ref[:n_slice, :] = weight_terms
    out_ref[n_slice:, :] = bias_terms


def fold_kernel(in_ref, out_ref, mark_ref):
    mark_ref[...] = jnp.zeros_like(mark_ref)
    total = in_ref[0].astype(F32)
    for s in range(1, in_ref.shape[0]):
        total += in_ref[s].astype(F32)
    out_ref[...] = total.astype(BF16)


def place_kernel(index_ref, *refs, n_slice):
    out_ref = refs[-1]
    offset = 0
    for ref in refs[:-1]:
        for k in range(ref.shape[0] // n_slice):
            first = pl.multiple_of((index_ref[0] ^ index_ref[1 + offset]) * n_slice, n_slice)
            out_ref[pl.ds(first, n_slice), :] = ref[k * n_slice : (k + 1) * n_slice, :]
            offset += 1


def last_kernel(in_ref, weight_ref, rows_ref):
    total = in_ref[0].astype(F32)
    for s in range(1, in_ref.shape[0]):
        total += in_ref[s].astype(F32)
    high = total.astype(BF16)
    low = (total - high.astype(F32)).astype(BF16)
    dims = (((1,), (1,)), ((), ()))
    product = lax.dot_general(high, weight_ref[...], dims, preferred_element_type=F32)
    product += lax.dot_general(low, weight_ref[...], dims, preferred_element_type=F32)
    rows_ref[...] = product.astype(BF16)


def call(kernel, out_shape, scratch=(), n_scalar=0, n_in=1, marked=False, out_space=pltpu.VMEM):
    smem = pl.BlockSpec(memory_space=pltpu.SMEM)
    vmem = pl.BlockSpec(memory_space=pltpu.VMEM)
    out_specs = pl.BlockSpec(memory_space=out_space)
    if marked:
        out_shape, out_specs = (out_shape, MARK), (out_specs, vmem)
    return pl.pallas_call(
        kernel,
        out_shape=out_shape,
        in_specs=[smem] * n_scalar + [vmem] * n_in,
        out_specs=out_specs,
        scratch_shapes=list(scratch),
        compiler_params=pltpu.CompilerParams(vmem_limit_bytes=VMEM_LIMIT),
    )


def swap(value, axis):
    return lax.all_to_all(value, axis, split_axis=0, concat_axis=0, tiled=True)


def trade(value, axis, bit):
    return lax.ppermute(value, axis, [(i, i ^ bit) for i in range(lax.axis_size(axis))])


def body(grad_out, relu_mask, aggregated, weight, adj_blocks, block_pos, block_live):
    blk, n_feat = grad_out.shape
    n_zh, n_y, n_zl, n_x, n_core = (lax.axis_size(a) for a in ("zh", "y", "zl", "x", "core"))
    n_rows = n_zl * blk
    n_pair = n_feat // (n_zl * n_x)
    n_slice = n_pair // n_core
    n_terms = n_slice + 8
    grad_pre = grad_out * relu_mask.astype(BF16)
    columns = aggregated.T.reshape(n_zl, n_x, n_pair, blk).transpose(0, 2, 1, 3)
    columns = columns.reshape(n_zl, n_pair, n_x * blk)
    sent = jnp.concatenate([jnp.broadcast_to(grad_pre, (n_zl, blk, n_feat)), columns], axis=1)
    got = swap(sent, "zl")
    rows = got[:, :blk].reshape(n_rows, n_feat)
    columns = got[:, blk:].reshape(n_zl, n_pair, n_x, blk).transpose(2, 1, 0, 3)
    columns = columns.reshape(n_x, n_pair, n_rows)
    sent = jnp.concatenate([jnp.broadcast_to(rows, (n_x, n_rows, n_feat)), columns], axis=1)
    own = swap(sent, "x")
    other = lax.ppermute(own, "core", [(0, 1), (1, 0)])
    core = lax.axis_index("core").astype(jnp.int32).reshape(1)
    slots = adj_blocks.shape[2]
    group = max(d for d in range(1, 9) if slots % d == 0)
    sent, mark = call(
        functools.partial(tile_kernel, group=group, n_x=n_x),
        jax.ShapeDtypeStruct((n_y, n_zh * blk, n_feat), BF16),
        scratch=[
            pltpu.VMEM((n_zh * n_y, blk, n_feat), F32),
            pltpu.VMEM((n_y, n_zh * blk, n_feat), BF16),
            pltpu.SemaphoreType.DMA((n_y,)),
        ],
        out_space=pltpu.HBM,
        marked=True,
        n_scalar=3,
        n_in=3,
    )(block_pos.reshape(-1), block_live.reshape(-1), core, adj_blocks[0, 0], own, other)
    later, _ = lax.optimization_barrier((core, mark))
    terms = call(
        functools.partial(terms_kernel, n_rows=n_rows),
        jax.ShapeDtypeStruct((n_terms, n_feat), F32),
        n_scalar=1,
        n_in=2,
    )(later, own, other)
    for bit in (1, 2):
        terms = terms + trade(terms, "zh", bit)
    factor = 1.0 / math.sqrt(blk * n_zh * n_y * n_zl * n_x * n_core)
    terms = terms * factor
    slices, bias = terms[:n_slice], terms[n_slice:]
    offsets = [0]
    for bit in (1, 2):
        slices = jnp.concatenate([slices, trade(slices, "zl", bit)], axis=0)
        offsets += [o ^ (bit * n_x * n_core) for o in offsets]
    terms = jnp.concatenate([slices, bias], axis=0)
    got = swap(sent, "y")
    sent, mark = call(fold_kernel, jax.ShapeDtypeStruct((n_zh * blk, n_feat), BF16), marked=True)(got)
    terms, _ = lax.optimization_barrier((terms, mark))
    for bit in (1, 2):
        terms = terms + trade(terms, "y", bit)
    pieces = [terms[: n_zl * n_slice]]
    for axis, bit, stride in (("x", 1, n_core), ("x", 2, n_core), ("core", 1, 1)):
        pieces.append(trade(jnp.concatenate(pieces, axis=0), axis, bit))
        offsets += [o ^ (bit * stride) for o in offsets]
    mine = lax.axis_index(("zl", "x", "core")).astype(jnp.int32)
    place = functools.partial(place_kernel, n_slice=n_slice)
    grad_weight = call(place, jax.ShapeDtypeStruct((n_feat, n_feat), F32), n_scalar=1, n_in=len(pieces))(
        jnp.concatenate([mine.reshape(1), jnp.array(offsets, jnp.int32)]), *pieces
    )
    got = swap(sent.reshape(n_zh, blk, n_feat), "zh")
    out_rows = call(last_kernel, jax.ShapeDtypeStruct((blk, n_feat), BF16), n_in=2)(got, weight)
    return out_rows[None], grad_weight, terms[n_zl * n_slice]


def solution(mesh):
    fine = Mesh(mesh.devices.reshape(4, 4, 4, 4, 2), ("zh", "y", "zl", "x", "core"))
    row, col = ("zh", "y"), ("zl", "x", "core")
    return jax.shard_map(
        body,
        mesh=fine,
        in_specs=(
            P(row + col, None),
            P(row + col, None),
            P(row + col, None),
            P(),
            P(row, col, None, None, None),
            P(row, col, None),
            P(row, col),
        ),
        out_specs=(P(col, row, None), P(), P()),
        check_vma=False,
    )
```

```python
import functools
import math

import jax
import jax.numpy as jnp
from jax import lax
from jax.experimental import pallas as pl
from jax.experimental.pallas import tpu as pltpu
from jax.sharding import Mesh, PartitionSpec as P

F32 = jnp.float32
BF16 = jnp.bfloat16
MARK = jax.ShapeDtypeStruct((8, 128), F32)
VMEM_LIMIT = 48 * 1024 * 1024


def tile_kernel(pos_ref, live_ref, core_ref, blocks_ref, own_ref, other_ref, out_ref, mark_ref, acc_ref, low_ref, sems, *, group, n_x):
    n_y, width, _ = out_ref.shape
    blk = blocks_ref.shape[-1]
    tile_cols = acc_ref.shape[0]
    acc_ref[...] = jnp.zeros_like(acc_ref)
    my_core = core_ref[0]
    live = live_ref[0]

    def add_group(turn, carry):
        found = []
        for k in range(group):
            slot = turn * group + k
            position = pos_ref[slot]
            source = position // tile_cols
            first = pl.multiple_of(source // (2 * n_x) * blk, blk)
            x_part = (source // 2) % n_x
            rows = jnp.where(
                source % 2 == my_core, own_ref[x_part, pl.ds(first, blk), :], other_ref[x_part, pl.ds(first, blk), :]
            )
            block = blocks_ref[slot]
            block = jnp.where(slot < live, block, jnp.zeros_like(block))
            product = lax.dot_general(block, rows, (((0,), (0,)), ((), ())), preferred_element_type=F32)
            found.append((position % tile_cols, product))
        for column, product in found:
            acc_ref[column] += product
        return carry

    lax.fori_loop(0, (live + group - 1) // group, add_group, 0)
    copies = []
    for y in range(n_y):
        for z in range(width // blk):
            low_ref[y, z * blk : (z + 1) * blk, :] = acc_ref[z * n_y + y].astype(BF16)
        copies.append(pltpu.make_async_copy(low_ref.at[y], out_ref.at[y], sems.at[y]))
        copies[-1].start()
    mark_ref[...] = jnp.zeros_like(mark_ref)
    for copy in copies:
        copy.wait()


def terms_kernel(place_ref, got_ref, keep_ref, send_ref, sum_ref, *, blk):
    n_src, width, n_feat = got_ref.shape
    n_y = n_feat // blk
    n_pair = width - blk
    n_slice = n_pair // 2
    ones = jnp.ones((8, blk), BF16)
    bias_terms = jnp.zeros((8, n_feat), F32)
    for s in range(n_src):
        bias_terms += jnp.dot(ones, got_ref[s, :blk, :], preferred_element_type=F32)
    for y in range(n_y):
        total = jnp.zeros((n_pair, n_feat), F32)
        for s in range(n_src):
            features = got_ref[s, blk:, y * blk : (y + 1) * blk]
            total += jnp.dot(features, got_ref[s, :blk, :], preferred_element_type=F32)
        sum_ref[y] = total
    mine, my_y = place_ref[0], place_ref[1]
    for ref, core in ((keep_ref, mine), (send_ref, 1 - mine)):
        first = pl.multiple_of(core * n_slice, n_slice)
        for y in range(n_y):
            ref[y * n_slice : (y + 1) * n_slice, :] = sum_ref[my_y ^ y, pl.ds(first, n_slice), :]
        ref[n_y * n_slice :, :] = bias_terms


def fold_kernel(in_ref, out_ref, mark_ref):
    mark_ref[...] = jnp.zeros_like(mark_ref)
    total = in_ref[0].astype(F32)
    for s in range(1, in_ref.shape[0]):
        total += in_ref[s].astype(F32)
    out_ref[...] = total.astype(BF16)


def place_kernel(index_ref, *refs, n_slice):
    out_ref = refs[-1]
    offset = 0
    for ref in refs[:-1]:
        for k in range(ref.shape[0] // n_slice):
            first = pl.multiple_of((index_ref[0] ^ index_ref[1 + offset]) * n_slice, n_slice)
            out_ref[pl.ds(first, n_slice), :] = ref[k * n_slice : (k + 1) * n_slice, :]
            offset += 1


def last_kernel(in_ref, weight_ref, rows_ref):
    total = in_ref[0].astype(F32)
    for s in range(1, in_ref.shape[0]):
        total += in_ref[s].astype(F32)
    high = total.astype(BF16)
    low = (total - high.astype(F32)).astype(BF16)
    dims = (((1,), (1,)), ((), ()))
    product = lax.dot_general(high, weight_ref[...], dims, preferred_element_type=F32)
    product += lax.dot_general(low, weight_ref[...], dims, preferred_element_type=F32)
    rows_ref[...] = product.astype(BF16)


def call(kernel, out_shape, scratch=(), n_scalar=0, n_in=1, marked=False, out_space=pltpu.VMEM):
    smem = pl.BlockSpec(memory_space=pltpu.SMEM)
    vmem = pl.BlockSpec(memory_space=pltpu.VMEM)
    out_specs = jax.tree.map(lambda _: pl.BlockSpec(memory_space=out_space), out_shape)
    if marked:
        out_shape, out_specs = (out_shape, MARK), (out_specs, vmem)
    return pl.pallas_call(
        kernel,
        out_shape=out_shape,
        in_specs=[smem] * n_scalar + [vmem] * n_in,
        out_specs=out_specs,
        scratch_shapes=list(scratch),
        compiler_params=pltpu.CompilerParams(vmem_limit_bytes=VMEM_LIMIT),
    )


def swap(value, axis):
    return lax.all_to_all(value, axis, split_axis=0, concat_axis=0, tiled=True)


def trade(value, axis, bit):
    return lax.ppermute(value, axis, [(i, i ^ bit) for i in range(lax.axis_size(axis))])


def body(grad_out, relu_mask, aggregated, weight, adj_blocks, block_pos, block_live):
    blk, n_feat = grad_out.shape
    n_zh, n_y, n_zl, n_x, n_core = (lax.axis_size(a) for a in ("zh", "y", "zl", "x", "core"))
    n_rows = n_zl * blk
    n_pair = n_feat // (n_zl * n_y)
    n_slice = n_pair // n_core
    grad_pre = grad_out * relu_mask.astype(BF16)
    columns = aggregated.T.reshape(n_zl, n_y, n_pair, blk).transpose(0, 2, 1, 3)
    columns = columns.reshape(n_zl, n_pair, n_y * blk)
    sent = jnp.concatenate([jnp.broadcast_to(grad_pre, (n_zl, blk, n_feat)), columns], axis=1)
    got = swap(sent, "zl")
    core, y_index = (lax.axis_index(a).astype(jnp.int32).reshape(1) for a in ("core", "y"))
    half = jax.ShapeDtypeStruct((n_y * n_slice + 8, n_feat), F32)
    terms, away = call(
        functools.partial(terms_kernel, blk=blk),
        (half, half),
        scratch=[pltpu.VMEM((n_y, n_pair, n_feat), F32)],
        n_scalar=1,
    )(jnp.concatenate([core, y_index]), got)
    rows = got[:, :blk].reshape(n_rows, n_feat)
    own = swap(jnp.broadcast_to(rows, (n_x, n_rows, n_feat)), "x")
    terms = terms + trade(away, "core", 1)
    for bit, n in ((2, 2 * n_slice), (1, n_slice)):
        kept, away, bias = terms[:n], terms[n : 2 * n], terms[2 * n :]
        terms = jnp.concatenate([kept, bias], axis=0) + trade(jnp.concatenate([away, bias], axis=0), "y", bit)
    terms = terms + trade(terms, "zh", 1)
    own, terms = lax.optimization_barrier((own, terms))
    other = lax.ppermute(own, "core", [(0, 1), (1, 0)])
    slots = adj_blocks.shape[2]
    group = max(d for d in range(1, 9) if slots % d == 0)
    sent, mark = call(
        functools.partial(tile_kernel, group=group, n_x=n_x),
        jax.ShapeDtypeStruct((n_y, n_zh * blk, n_feat), BF16),
        scratch=[
            pltpu.VMEM((n_zh * n_y, blk, n_feat), F32),
            pltpu.VMEM((n_y, n_zh * blk, n_feat), BF16),
            pltpu.SemaphoreType.DMA((n_y,)),
        ],
        out_space=pltpu.HBM,
        marked=True,
        n_scalar=3,
        n_in=3,
    )(block_pos.reshape(-1), block_live.reshape(-1), core, adj_blocks[0, 0], own, other)
    terms, _ = lax.optimization_barrier((terms, mark))
    terms = terms + trade(terms, "zh", 2)
    factor = 1.0 / math.sqrt(blk * n_zh * n_y * n_zl * n_x * n_core)
    terms = terms * factor
    slices, bias = terms[:n_slice], terms[n_slice:]
    offsets = [0]
    for bit in (1, 2):
        slices = jnp.concatenate([slices, trade(slices, "zl", bit)], axis=0)
        offsets += [o ^ (bit * n_y * n_core) for o in offsets]
    terms = jnp.concatenate([slices, bias], axis=0)
    got = swap(sent, "y")
    sent, mark = call(fold_kernel, jax.ShapeDtypeStruct((n_zh * blk, n_feat), BF16), marked=True)(got)
    terms, _ = lax.optimization_barrier((terms, mark))
    for bit in (1, 2):
        terms = terms + trade(terms, "x", bit)
    pieces = [terms[: n_zl * n_slice]]
    for axis, bit, stride in (("y", 1, n_core), ("y", 2, n_core), ("core", 1, 1)):
        pieces.append(trade(jnp.concatenate(pieces, axis=0), axis, bit))
        offsets += [o ^ (bit * stride) for o in offsets]
    mine = lax.axis_index(("zl", "y", "core")).astype(jnp.int32)
    place = functools.partial(place_kernel, n_slice=n_slice)
    grad_weight = call(place, jax.ShapeDtypeStruct((n_feat, n_feat), F32), n_scalar=1, n_in=len(pieces))(
        jnp.concatenate([mine.reshape(1), jnp.array(offsets, jnp.int32)]), *pieces
    )
    got = swap(sent.reshape(n_zh, blk, n_feat), "zh")
    out_rows = call(last_kernel, jax.ShapeDtypeStruct((blk, n_feat), BF16), n_in=2)(got, weight)
    return out_rows[None], grad_weight, terms[n_zl * n_slice]


def solution(mesh):
    fine = Mesh(mesh.devices.reshape(4, 4, 4, 4, 2), ("zh", "y", "zl", "x", "core"))
    row, col = ("zh", "y"), ("zl", "x", "core")
    return jax.shard_map(
        body,
        mesh=fine,
        in_specs=(
            P(row + col, None),
            P(row + col, None),
            P(row + col, None),
            P(),
            P(row, col, None, None, None),
            P(row, col, None),
            P(row, col),
        ),
        out_specs=(P(col, row, None), P(), P()),
        check_vma=False,
    )
```

```python
import functools
import math

import jax
import jax.numpy as jnp
from jax import lax
from jax.experimental import pallas as pl
from jax.experimental.pallas import tpu as pltpu
from jax.sharding import Mesh, PartitionSpec as P

F32 = jnp.float32
BF16 = jnp.bfloat16
MARK = jax.ShapeDtypeStruct((8, 128), F32)
VMEM_LIMIT = 24 * 1024 * 1024


def tile_kernel(pos_ref, live_ref, core_ref, blocks_ref, own_ref, other_ref, out_ref, mark_ref, acc_ref, low_ref, sems, *, group, n_x):
    n_y, width, _ = out_ref.shape
    blk = blocks_ref.shape[-1]
    tile_cols = acc_ref.shape[0]
    acc_ref[...] = jnp.zeros_like(acc_ref)
    my_core = core_ref[0]
    live = live_ref[0]

    def add_group(turn, carry):
        found = []
        for k in range(group):
            slot = turn * group + k
            position = pos_ref[slot]
            source = position // tile_cols
            first = pl.multiple_of(source // (2 * n_x) * blk, blk)
            x_part = (source // 2) % n_x
            rows = jnp.where(
                source % 2 == my_core, own_ref[x_part, pl.ds(first, blk), :], other_ref[x_part, pl.ds(first, blk), :]
            )
            block = blocks_ref[slot]
            block = jnp.where(slot < live, block, jnp.zeros_like(block))
            product = lax.dot_general(block, rows, (((0,), (0,)), ((), ())), preferred_element_type=F32)
            found.append((position % tile_cols, product))
        for column, product in found:
            acc_ref[column] += product
        return carry

    lax.fori_loop(0, (live + group - 1) // group, add_group, 0)
    copies = []
    for y in range(n_y):
        for z in range(width // blk):
            low_ref[y, z * blk : (z + 1) * blk, :] = acc_ref[z * n_y + y].astype(BF16)
        copies.append(pltpu.make_async_copy(low_ref.at[y], out_ref.at[y], sems.at[y]))
        copies[-1].start()
    mark_ref[...] = jnp.zeros_like(mark_ref)
    for copy in copies:
        copy.wait()


def terms_kernel(place_ref, got_ref, keep_ref, send_ref, sum_ref, *, blk):
    n_src, width, n_feat = got_ref.shape
    n_y = n_feat // blk
    n_pair = width - blk
    n_slice = n_pair // 2
    ones = jnp.ones((8, blk), BF16)
    bias_terms = jnp.zeros((8, n_feat), F32)
    for s in range(n_src):
        bias_terms += jnp.dot(ones, got_ref[s, :blk, :], preferred_element_type=F32)
    for y in range(n_y):
        total = jnp.zeros((n_pair, n_feat), F32)
        for s in range(n_src):
            features = got_ref[s, blk:, y * blk : (y + 1) * blk]
            total += jnp.dot(features, got_ref[s, :blk, :], preferred_element_type=F32)
        sum_ref[y] = total
    mine, my_y = place_ref[0], place_ref[1]
    for ref, core in ((keep_ref, mine), (send_ref, 1 - mine)):
        first = pl.multiple_of(core * n_slice, n_slice)
        for y in range(n_y):
            ref[y * n_slice : (y + 1) * n_slice, :] = sum_ref[my_y ^ y, pl.ds(first, n_slice), :]
        ref[n_y * n_slice :, :] = bias_terms


def fold_kernel(in_ref, out_ref, mark_ref):
    mark_ref[...] = jnp.zeros_like(mark_ref)
    total = in_ref[0].astype(F32)
    for s in range(1, in_ref.shape[0]):
        total += in_ref[s].astype(F32)
    out_ref[...] = total.astype(BF16)


def place_kernel(index_ref, *refs, n_slice):
    out_ref = refs[-1]
    offset = 0
    for ref in refs[:-1]:
        for k in range(ref.shape[0] // n_slice):
            first = pl.multiple_of((index_ref[0] ^ index_ref[1 + offset]) * n_slice, n_slice)
            out_ref[pl.ds(first, n_slice), :] = ref[k * n_slice : (k + 1) * n_slice, :].astype(F32)
            offset += 1


def last_kernel(in_ref, weight_ref, rows_ref):
    total = in_ref[0].astype(F32)
    for s in range(1, in_ref.shape[0]):
        total += in_ref[s].astype(F32)
    high = total.astype(BF16)
    low = (total - high.astype(F32)).astype(BF16)
    dims = (((1,), (1,)), ((), ()))
    product = lax.dot_general(high, weight_ref[...], dims, preferred_element_type=F32)
    product += lax.dot_general(low, weight_ref[...], dims, preferred_element_type=F32)
    rows_ref[...] = product.astype(BF16)


def call(kernel, out_shape, scratch=(), n_scalar=0, n_in=1, marked=False, out_space=pltpu.VMEM):
    smem = pl.BlockSpec(memory_space=pltpu.SMEM)
    vmem = pl.BlockSpec(memory_space=pltpu.VMEM)
    out_specs = jax.tree.map(lambda _: pl.BlockSpec(memory_space=out_space), out_shape)
    if marked:
        out_shape, out_specs = (out_shape, MARK), (out_specs, vmem)
    return pl.pallas_call(
        kernel,
        out_shape=out_shape,
        in_specs=[smem] * n_scalar + [vmem] * n_in,
        out_specs=out_specs,
        scratch_shapes=list(scratch),
        compiler_params=pltpu.CompilerParams(vmem_limit_bytes=VMEM_LIMIT),
    )


def swap(value, axis):
    return lax.all_to_all(value, axis, split_axis=0, concat_axis=0, tiled=True)


def trade(value, axis, bit):
    return lax.ppermute(value, axis, [(i, i ^ bit) for i in range(lax.axis_size(axis))])


def body(grad_out, relu_mask, aggregated, weight, adj_blocks, block_pos, block_live):
    blk, n_feat = grad_out.shape
    n_zh, n_y, n_zl, n_x, n_core = (lax.axis_size(a) for a in ("zh", "y", "zl", "x", "core"))
    n_rows = n_zl * blk
    n_pair = n_feat // (n_zl * n_y)
    n_slice = n_pair // n_core
    grad_pre = grad_out * relu_mask.astype(BF16)
    columns = aggregated.T.reshape(n_zl, n_y, n_pair, blk).transpose(0, 2, 1, 3)
    columns = columns.reshape(n_zl, n_pair, n_y * blk)
    sent = jnp.concatenate([jnp.broadcast_to(grad_pre, (n_zl, blk, n_feat)), columns], axis=1)
    got = swap(sent, "zl")
    core, y_index = (lax.axis_index(a).astype(jnp.int32).reshape(1) for a in ("core", "y"))
    half = jax.ShapeDtypeStruct((n_y * n_slice + 8, n_feat), F32)
    terms, away = call(
        functools.partial(terms_kernel, blk=blk),
        (half, half),
        scratch=[pltpu.VMEM((n_y, n_pair, n_feat), F32)],
        n_scalar=1,
    )(jnp.concatenate([core, y_index]), got)
    rows = got[:, :blk].reshape(n_rows, n_feat)
    own = swap(jnp.broadcast_to(rows, (n_x, n_rows, n_feat)), "x")
    terms = terms + trade(away, "core", 1)
    for bit, n in ((2, 2 * n_slice), (1, n_slice)):
        kept, away, bias = terms[:n], terms[n : 2 * n], terms[2 * n :]
        terms = jnp.concatenate([kept, bias], axis=0) + trade(jnp.concatenate([away, bias], axis=0), "y", bit)
    terms = terms + trade(terms, "zh", 1)
    own, terms = lax.optimization_barrier((own, terms))
    other = lax.ppermute(own, "core", [(0, 1), (1, 0)])
    terms = terms + trade(terms, "x", 1)
    later, terms = lax.optimization_barrier((core, terms))
    terms = terms + trade(terms, "x", 2)
    slots = adj_blocks.shape[2]
    group = max(d for d in range(1, 9) if slots % d == 0)
    sent, mark = call(
        functools.partial(tile_kernel, group=group, n_x=n_x),
        jax.ShapeDtypeStruct((n_y, n_zh * blk, n_feat), BF16),
        scratch=[
            pltpu.VMEM((n_zh * n_y, blk, n_feat), F32),
            pltpu.VMEM((n_y, n_zh * blk, n_feat), BF16),
            pltpu.SemaphoreType.DMA((n_y,)),
        ],
        out_space=pltpu.HBM,
        marked=True,
        n_scalar=3,
        n_in=3,
    )(block_pos.reshape(-1), block_live.reshape(-1), later, adj_blocks[0, 0], own, other)
    terms, sent = lax.optimization_barrier((terms, sent))
    terms = terms + trade(terms, "zh", 2)
    factor = 1.0 / math.sqrt(blk * n_zh * n_y * n_zl * n_x * n_core)
    terms = terms * factor
    slices = terms[:n_slice].astype(BF16)
    offsets = [0]
    for bit in (1, 2):
        slices = jnp.concatenate([slices, trade(slices, "zl", bit)], axis=0)
        offsets += [o ^ (bit * n_y * n_core) for o in offsets]
    got = swap(sent, "y")
    sent, mark = call(fold_kernel, jax.ShapeDtypeStruct((n_zh * blk, n_feat), BF16), marked=True)(got)
    slices, sent = lax.optimization_barrier((slices, sent))
    pieces = [slices]
    for axis, bit, stride in (("y", 2, n_core), ("y", 1, n_core), ("core", 1, 1)):
        pieces.append(trade(jnp.concatenate(pieces, axis=0), axis, bit))
        offsets += [o ^ (bit * stride) for o in offsets]
    mine = lax.axis_index(("zl", "y", "core")).astype(jnp.int32)
    place = functools.partial(place_kernel, n_slice=n_slice)
    grad_weight = call(place, jax.ShapeDtypeStruct((n_feat, n_feat), F32), n_scalar=1, n_in=len(pieces))(
        jnp.concatenate([mine.reshape(1), jnp.array(offsets, jnp.int32)]), *pieces
    )
    got = swap(sent.reshape(n_zh, blk, n_feat), "zh")
    out_rows = call(last_kernel, jax.ShapeDtypeStruct((blk, n_feat), BF16), n_in=2)(got, weight)
    return out_rows[None], grad_weight, terms[n_slice]


def solution(mesh):
    fine = Mesh(mesh.devices.reshape(4, 4, 4, 4, 2), ("zh", "y", "zl", "x", "core"))
    row, col = ("zh", "y"), ("zl", "x", "core")
    return jax.shard_map(
        body,
        mesh=fine,
        in_specs=(
            P(row + col, None),
            P(row + col, None),
            P(row + col, None),
            P(),
            P(row, col, None, None, None),
            P(row, col, None),
            P(row, col),
        ),
        out_specs=(P(col, row, None), P(), P()),
        check_vma=False,
    )
```

```python
import functools
import math

import jax
import jax.numpy as jnp
from jax import lax
from jax.experimental import pallas as pl
from jax.experimental.pallas import tpu as pltpu
from jax.sharding import Mesh, PartitionSpec as P

F32 = jnp.float32
BF16 = jnp.bfloat16
MARK = jax.ShapeDtypeStruct((8, 128), F32)
VMEM_LIMIT = 24 * 1024 * 1024


def tile_kernel(pos_ref, live_ref, core_ref, blocks_ref, own_ref, other_ref, out_ref, mark_ref, acc_ref, low_ref, sems, *, group, n_x):
    n_y, width, _ = out_ref.shape
    blk = blocks_ref.shape[-1]
    tile_cols = acc_ref.shape[0]
    acc_ref[...] = jnp.zeros_like(acc_ref)
    my_core = core_ref[0]
    live = live_ref[0]

    def add_group(turn, carry):
        found = []
        for k in range(group):
            slot = turn * group + k
            position = pos_ref[slot]
            source = position // tile_cols
            first = pl.multiple_of(source // (2 * n_x) * blk, blk)
            x_part = (source // 2) % n_x
            rows = jnp.where(
                source % 2 == my_core, own_ref[x_part, pl.ds(first, blk), :], other_ref[x_part, pl.ds(first, blk), :]
            )
            block = blocks_ref[slot]
            block = jnp.where(slot < live, block, jnp.zeros_like(block))
            product = lax.dot_general(block, rows, (((0,), (0,)), ((), ())), preferred_element_type=F32)
            found.append((position % tile_cols, product))
        for column, product in found:
            acc_ref[column] += product
        return carry

    lax.fori_loop(0, (live + group - 1) // group, add_group, 0)
    copies = []
    for y in range(n_y):
        for z in range(width // blk):
            low_ref[y, z * blk : (z + 1) * blk, :] = acc_ref[z * n_y + y].astype(BF16)
        copies.append(pltpu.make_async_copy(low_ref.at[y], out_ref.at[y], sems.at[y]))
        copies[-1].start()
    mark_ref[...] = jnp.zeros_like(mark_ref)
    for copy in copies:
        copy.wait()


def terms_kernel(place_ref, got_ref, keep_ref, send_ref, sum_ref, *, blk):
    n_src, width, n_feat = got_ref.shape
    n_y = n_feat // blk
    n_pair = width - blk
    n_slice = n_pair // 2
    ones = jnp.ones((8, blk), BF16)
    bias_terms = jnp.zeros((8, n_feat), F32)
    for s in range(n_src):
        bias_terms += jnp.dot(ones, got_ref[s, :blk, :], preferred_element_type=F32)
    for y in range(n_y):
        total = jnp.zeros((n_pair, n_feat), F32)
        for s in range(n_src):
            features = got_ref[s, blk:, y * blk : (y + 1) * blk]
            total += jnp.dot(features, got_ref[s, :blk, :], preferred_element_type=F32)
        sum_ref[y] = total
    mine, my_y = place_ref[0], place_ref[1]
    for ref, core in ((keep_ref, mine), (send_ref, 1 - mine)):
        first = pl.multiple_of(core * n_slice, n_slice)
        for y in range(n_y):
            ref[y * n_slice : (y + 1) * n_slice, :] = sum_ref[my_y ^ y, pl.ds(first, n_slice), :]
        ref[n_y * n_slice :, :] = bias_terms


def fold_kernel(in_ref, out_ref, mark_ref):
    mark_ref[...] = jnp.zeros_like(mark_ref)
    total = in_ref[0].astype(F32)
    for s in range(1, in_ref.shape[0]):
        total += in_ref[s].astype(F32)
    out_ref[...] = total.astype(BF16)


def place_kernel(index_ref, *refs, n_slice):
    out_ref = refs[-1]
    offset = 0
    for ref in refs[:-1]:
        for k in range(ref.shape[0] // n_slice):
            first = pl.multiple_of((index_ref[0] ^ index_ref[1 + offset]) * n_slice, n_slice)
            out_ref[pl.ds(first, n_slice), :] = ref[k * n_slice : (k + 1) * n_slice, :].astype(F32)
            offset += 1


def last_kernel(in_ref, weight_ref, rows_ref):
    total = in_ref[0].astype(F32)
    for s in range(1, in_ref.shape[0]):
        total += in_ref[s].astype(F32)
    high = total.astype(BF16)
    low = (total - high.astype(F32)).astype(BF16)
    dims = (((1,), (1,)), ((), ()))
    product = lax.dot_general(high, weight_ref[...], dims, preferred_element_type=F32)
    product += lax.dot_general(low, weight_ref[...], dims, preferred_element_type=F32)
    rows_ref[...] = product.astype(BF16)


def call(kernel, out_shape, scratch=(), n_scalar=0, n_in=1, marked=False, out_space=pltpu.VMEM, cost=None):
    smem = pl.BlockSpec(memory_space=pltpu.SMEM)
    vmem = pl.BlockSpec(memory_space=pltpu.VMEM)
    out_specs = jax.tree.map(lambda _: pl.BlockSpec(memory_space=out_space), out_shape)
    if marked:
        out_shape, out_specs = (out_shape, MARK), (out_specs, vmem)
    return pl.pallas_call(
        kernel,
        out_shape=out_shape,
        in_specs=[smem] * n_scalar + [vmem] * n_in,
        out_specs=out_specs,
        scratch_shapes=list(scratch),
        cost_estimate=cost,
        compiler_params=pltpu.CompilerParams(vmem_limit_bytes=VMEM_LIMIT),
    )


def swap(value, axis):
    return lax.all_to_all(value, axis, split_axis=0, concat_axis=0, tiled=True)


def trade(value, axis, bit):
    return lax.ppermute(value, axis, [(i, i ^ bit) for i in range(lax.axis_size(axis))])


def body(grad_out, relu_mask, aggregated, weight, adj_blocks, block_pos, block_live):
    blk, n_feat = grad_out.shape
    n_zh, n_y, n_zl, n_x, n_core = (lax.axis_size(a) for a in ("zh", "y", "zl", "x", "core"))
    n_rows = n_zl * blk
    n_pair = n_feat // (n_zl * n_y)
    n_slice = n_pair // n_core
    grad_pre = grad_out * relu_mask.astype(BF16)
    columns = aggregated.T.reshape(n_zl, n_y, n_pair, blk).transpose(0, 2, 1, 3)
    columns = columns.reshape(n_zl, n_pair, n_y * blk)
    sent = jnp.concatenate([jnp.broadcast_to(grad_pre, (n_zl, blk, n_feat)), columns], axis=1)
    got = swap(sent, "zl")
    core, y_index = (lax.axis_index(a).astype(jnp.int32).reshape(1) for a in ("core", "y"))
    half = jax.ShapeDtypeStruct((n_y * n_slice + 8, n_feat), F32)
    terms, away = call(
        functools.partial(terms_kernel, blk=blk),
        (half, half),
        scratch=[pltpu.VMEM((n_y, n_pair, n_feat), F32)],
        n_scalar=1,
    )(jnp.concatenate([core, y_index]), got)
    rows = got[:, :blk].reshape(n_rows, n_feat)
    own = swap(jnp.broadcast_to(rows, (n_x, n_rows, n_feat)), "x")
    terms = terms + trade(away, "core", 1)
    for bit, n in ((2, 2 * n_slice), (1, n_slice)):
        kept, away, bias = terms[:n], terms[n : 2 * n], terms[2 * n :]
        terms = jnp.concatenate([kept, bias], axis=0) + trade(jnp.concatenate([away, bias], axis=0), "y", bit)
    own, terms = lax.optimization_barrier((own, terms))
    other = lax.ppermute(own, "core", [(0, 1), (1, 0)])
    terms = swap(jnp.broadcast_to(terms, (n_zh,) + terms.shape), "zh")
    slots = adj_blocks.shape[2]
    group = max(d for d in range(1, 9) if slots % d == 0)
    sent, mark = call(
        functools.partial(tile_kernel, group=group, n_x=n_x),
        jax.ShapeDtypeStruct((n_y, n_zh * blk, n_feat), BF16),
        scratch=[
            pltpu.VMEM((n_zh * n_y, blk, n_feat), F32),
            pltpu.VMEM((n_y, n_zh * blk, n_feat), BF16),
            pltpu.SemaphoreType.DMA((n_y,)),
        ],
        out_space=pltpu.HBM,
        marked=True,
        cost=pl.CostEstimate(
            flops=2 * slots * blk * blk * n_feat,
            transcendentals=0,
            bytes_accessed=8 * slots * blk * n_feat,
        ),
        n_scalar=3,
        n_in=3,
    )(block_pos.reshape(-1), block_live.reshape(-1), core, adj_blocks[0, 0], own, other)
    terms, sent = lax.optimization_barrier((terms, sent))
    terms = terms.sum(axis=0)
    for bit in (1, 2):
        terms = terms + trade(terms, "x", bit)
    factor = 1.0 / math.sqrt(blk * n_zh * n_y * n_zl * n_x * n_core)
    terms = terms * factor
    slices = terms[:n_slice].astype(BF16)
    offsets = [0]
    for bit in (1, 2):
        slices = jnp.concatenate([slices, trade(slices, "zl", bit)], axis=0)
        offsets += [o ^ (bit * n_y * n_core) for o in offsets]
    got = swap(sent, "y")
    sent, mark = call(fold_kernel, jax.ShapeDtypeStruct((n_zh * blk, n_feat), BF16), marked=True)(got)
    slices, sent = lax.optimization_barrier((slices, sent))
    pieces = [slices]
    for axis, bit, stride in (("y", 2, n_core), ("y", 1, n_core), ("core", 1, 1)):
        pieces.append(trade(jnp.concatenate(pieces, axis=0), axis, bit))
        offsets += [o ^ (bit * stride) for o in offsets]
    mine = lax.axis_index(("zl", "y", "core")).astype(jnp.int32)
    place = functools.partial(place_kernel, n_slice=n_slice)
    grad_weight = call(place, jax.ShapeDtypeStruct((n_feat, n_feat), F32), n_scalar=1, n_in=len(pieces))(
        jnp.concatenate([mine.reshape(1), jnp.array(offsets, jnp.int32)]), *pieces
    )
    got = swap(sent.reshape(n_zh, blk, n_feat), "zh")
    out_rows = call(last_kernel, jax.ShapeDtypeStruct((blk, n_feat), BF16), n_in=2)(got, weight)
    return out_rows[None], grad_weight, terms[n_slice]


def solution(mesh):
    fine = Mesh(mesh.devices.reshape(4, 4, 4, 4, 2), ("zh", "y", "zl", "x", "core"))
    row, col = ("zh", "y"), ("zl", "x", "core")
    return jax.shard_map(
        body,
        mesh=fine,
        in_specs=(
            P(row + col, None),
            P(row + col, None),
            P(row + col, None),
            P(),
            P(row, col, None, None, None),
            P(row, col, None),
            P(row, col),
        ),
        out_specs=(P(col, row, None), P(), P()),
        check_vma=False,
    )
```

```python
import functools
import math

import jax
import jax.numpy as jnp
from jax import lax
from jax.experimental import pallas as pl
from jax.experimental.pallas import tpu as pltpu
from jax.sharding import Mesh, PartitionSpec as P

F32 = jnp.float32
BF16 = jnp.bfloat16
MARK = jax.ShapeDtypeStruct((8, 128), F32)
VMEM_LIMIT = 24 * 1024 * 1024
TILE_LIMIT = 54 * 1024 * 1024


def tile_kernel(pos_ref, live_ref, core_ref, blocks_ref, own_ref, other_ref, out_ref, mark_ref, acc_ref, low_ref, near_ref, sems, near_sems, *, group, n_x):
    n_y, width, _ = out_ref.shape
    blk = blocks_ref.shape[-1]
    tile_cols = acc_ref.shape[0]
    my_core = core_ref[0]
    live = live_ref[0]
    turns = (live + group - 1) // group

    def fetch(turn):
        part = pl.ds(turn * group, group)
        return pltpu.make_async_copy(blocks_ref.at[part], near_ref.at[part], near_sems.at[turn])

    lax.fori_loop(0, turns, lambda turn, carry: (fetch(turn).start(), carry)[1], 0)
    acc_ref[...] = jnp.zeros_like(acc_ref)

    def add_group(turn, carry):
        fetch(turn).wait()
        found = []
        for k in range(group):
            slot = turn * group + k
            position = pos_ref[slot]
            source = position // tile_cols
            first = pl.multiple_of(source // (2 * n_x) * blk, blk)
            x_part = (source // 2) % n_x
            rows = jnp.where(
                source % 2 == my_core, own_ref[x_part, pl.ds(first, blk), :], other_ref[x_part, pl.ds(first, blk), :]
            )
            block = near_ref[slot]
            block = jnp.where(slot < live, block, jnp.zeros_like(block))
            product = lax.dot_general(block, rows, (((0,), (0,)), ((), ())), preferred_element_type=F32)
            found.append((position % tile_cols, product))
        for column, product in found:
            acc_ref[column] += product
        return carry

    lax.fori_loop(0, turns, add_group, 0)
    copies = []
    for y in range(n_y):
        for z in range(width // blk):
            low_ref[y, z * blk : (z + 1) * blk, :] = acc_ref[z * n_y + y].astype(BF16)
        copies.append(pltpu.make_async_copy(low_ref.at[y], out_ref.at[y], sems.at[y]))
        copies[-1].start()
    mark_ref[...] = jnp.zeros_like(mark_ref)
    for copy in copies:
        copy.wait()


def terms_kernel(place_ref, got_ref, keep_ref, send_ref, sum_ref, *, blk):
    n_src, _, n_feat = got_ref.shape
    n_y, n_pair, _ = sum_ref.shape
    n_slice = n_pair // 2
    n_mine = n_y * n_pair
    ones = jnp.ones((8, blk), BF16)
    bias_terms = jnp.zeros((8, n_feat), F32)
    total = jnp.zeros((n_mine, n_feat), F32)
    for s in range(n_src):
        rows = got_ref[s, :blk, :]
        features = [got_ref[s, blk:, k * n_mine : (k + 1) * n_mine] for k in range(n_feat // n_mine)]
        features = jnp.concatenate(features, axis=0)
        total += lax.dot_general(features, rows, (((0,), (0,)), ((), ())), preferred_element_type=F32)
        bias_terms += jnp.dot(ones, rows, preferred_element_type=F32)
    for y in range(n_y):
        sum_ref[y] = total[y * n_pair : (y + 1) * n_pair]
    mine, my_y = place_ref[0], place_ref[1]
    for ref, core in ((keep_ref, mine), (send_ref, 1 - mine)):
        first = pl.multiple_of(core * n_slice, n_slice)
        for y in range(n_y):
            ref[y * n_slice : (y + 1) * n_slice, :] = sum_ref[my_y ^ y, pl.ds(first, n_slice), :]
        ref[n_y * n_slice :, :] = bias_terms


def fold_kernel(in_ref, out_ref, mark_ref):
    mark_ref[...] = jnp.zeros_like(mark_ref)
    total = in_ref[0].astype(F32)
    for s in range(1, in_ref.shape[0]):
        total += in_ref[s].astype(F32)
    out_ref[...] = total.astype(BF16)


def place_kernel(index_ref, *refs, n_slice):
    out_ref = refs[-1]
    offset = 0
    for ref in refs[:-1]:
        for k in range(ref.shape[0] // n_slice):
            first = pl.multiple_of((index_ref[0] ^ index_ref[1 + offset]) * n_slice, n_slice)
            out_ref[pl.ds(first, n_slice), :] = ref[k * n_slice : (k + 1) * n_slice, :].astype(F32)
            offset += 1


def last_kernel(in_ref, weight_ref, rows_ref):
    total = in_ref[0].astype(F32)
    for s in range(1, in_ref.shape[0]):
        total += in_ref[s].astype(F32)
    high = total.astype(BF16)
    low = (total - high.astype(F32)).astype(BF16)
    dims = (((1,), (1,)), ((), ()))
    product = lax.dot_general(high, weight_ref[...], dims, preferred_element_type=F32)
    product += lax.dot_general(low, weight_ref[...], dims, preferred_element_type=F32)
    rows_ref[...] = product.astype(BF16)


def call(kernel, out_shape, scratch=(), n_scalar=0, n_far=0, n_in=1, marked=False, limit=VMEM_LIMIT, out_space=pltpu.VMEM, cost=None):
    smem = pl.BlockSpec(memory_space=pltpu.SMEM)
    vmem = pl.BlockSpec(memory_space=pltpu.VMEM)
    out_specs = jax.tree.map(lambda _: pl.BlockSpec(memory_space=out_space), out_shape)
    if marked:
        out_shape, out_specs = (out_shape, MARK), (out_specs, vmem)
    return pl.pallas_call(
        kernel,
        out_shape=out_shape,
        in_specs=[smem] * n_scalar + [pl.BlockSpec(memory_space=pltpu.HBM)] * n_far + [vmem] * n_in,
        out_specs=out_specs,
        scratch_shapes=list(scratch),
        cost_estimate=cost,
        compiler_params=pltpu.CompilerParams(vmem_limit_bytes=limit),
    )


def swap(value, axis):
    return lax.all_to_all(value, axis, split_axis=0, concat_axis=0, tiled=True)


def trade(value, axis, bit):
    return lax.ppermute(value, axis, [(i, i ^ bit) for i in range(lax.axis_size(axis))])


def body(grad_out, relu_mask, aggregated, weight, adj_blocks, block_pos, block_live):
    blk, n_feat = grad_out.shape
    n_zh, n_y, n_zl, n_x, n_core = (lax.axis_size(a) for a in ("zh", "y", "zl", "x", "core"))
    n_rows = n_zl * blk
    n_pair = n_feat // (n_zl * n_y)
    n_slice = n_pair // n_core
    grad_pre = grad_out * relu_mask.astype(BF16)
    n_mine = n_feat // n_zl
    columns = aggregated.reshape(n_feat // n_mine, blk * n_mine // n_feat, n_zl, n_mine).transpose(2, 1, 0, 3)
    columns = columns.reshape(n_zl, blk * n_mine // n_feat, n_feat)
    sent = jnp.concatenate([jnp.broadcast_to(grad_pre, (n_zl, blk, n_feat)), columns], axis=1)
    got = swap(sent, "zl")
    core, y_index = (lax.axis_index(a).astype(jnp.int32).reshape(1) for a in ("core", "y"))
    half = jax.ShapeDtypeStruct((n_y * n_slice + 8, n_feat), F32)
    terms, away = call(
        functools.partial(terms_kernel, blk=blk),
        (half, half),
        scratch=[pltpu.VMEM((n_y, n_pair, n_feat), F32)],
        n_scalar=1,
    )(jnp.concatenate([core, y_index]), got)
    rows = got[:, :blk].reshape(n_rows, n_feat)
    own = swap(jnp.broadcast_to(rows, (n_x, n_rows, n_feat)), "x")
    terms = terms + trade(away, "core", 1)
    for bit, n in ((2, 2 * n_slice), (1, n_slice)):
        kept, away, bias = terms[:n], terms[n : 2 * n], terms[2 * n :]
        terms = jnp.concatenate([kept, bias], axis=0) + trade(jnp.concatenate([away, bias], axis=0), "y", bit)
    terms = terms + trade(terms, "zh", 1)
    own, terms = lax.optimization_barrier((own, terms))
    other = lax.ppermute(own, "core", [(0, 1), (1, 0)])
    terms = swap(jnp.broadcast_to(terms, (n_x,) + terms.shape), "x")
    slots = adj_blocks.shape[2]
    group = max(d for d in range(1, 9) if slots % d == 0)
    sent, mark = call(
        functools.partial(tile_kernel, group=group, n_x=n_x),
        jax.ShapeDtypeStruct((n_y, n_zh * blk, n_feat), BF16),
        scratch=[
            pltpu.VMEM((n_zh * n_y, blk, n_feat), F32),
            pltpu.VMEM((n_y, n_zh * blk, n_feat), BF16),
            pltpu.VMEM((slots, blk, blk), BF16),
            pltpu.SemaphoreType.DMA((n_y,)),
            pltpu.SemaphoreType.DMA((slots // group,)),
        ],
        n_far=1,
        limit=TILE_LIMIT,
        out_space=pltpu.HBM,
        marked=True,
        cost=pl.CostEstimate(
            flops=2 * slots * blk * blk * n_feat,
            transcendentals=0,
            bytes_accessed=8 * slots * blk * n_feat,
        ),
        n_scalar=3,
        n_in=2,
    )(block_pos.reshape(-1), block_live.reshape(-1), core, adj_blocks[0, 0], own, other)
    terms, sent = lax.optimization_barrier((terms, sent))
    terms = terms.sum(axis=0)
    terms = terms + trade(terms, "zh", 2)
    factor = 1.0 / math.sqrt(blk * n_zh * n_y * n_zl * n_x * n_core)
    terms = terms * factor
    slices = terms[:n_slice].astype(BF16)
    offsets = [0]
    for bit in (1, 2):
        slices = jnp.concatenate([slices, trade(slices, "zl", bit)], axis=0)
        offsets += [o ^ (bit * n_y * n_core) for o in offsets]
    got = swap(sent, "y")
    sent, mark = call(fold_kernel, jax.ShapeDtypeStruct((n_zh * blk, n_feat), BF16), marked=True)(got)
    slices, sent = lax.optimization_barrier((slices, sent))
    pieces = [slices]
    for axis, bit, stride in (("y", 2, n_core), ("y", 1, n_core), ("core", 1, 1)):
        pieces.append(trade(jnp.concatenate(pieces, axis=0), axis, bit))
        offsets += [o ^ (bit * stride) for o in offsets]
    mine = lax.axis_index(("zl", "y", "core")).astype(jnp.int32)
    place = functools.partial(place_kernel, n_slice=n_slice)
    grad_weight = call(place, jax.ShapeDtypeStruct((n_feat, n_feat), F32), n_scalar=1, n_in=len(pieces))(
        jnp.concatenate([mine.reshape(1), jnp.array(offsets, jnp.int32)]), *pieces
    )
    got = swap(sent.reshape(n_zh, blk, n_feat), "zh")
    out_rows = call(last_kernel, jax.ShapeDtypeStruct((blk, n_feat), BF16), n_in=2)(got, weight)
    return out_rows[None], grad_weight, terms[n_slice]


def solution(mesh):
    fine = Mesh(mesh.devices.reshape(4, 4, 4, 4, 2), ("zh", "y", "zl", "x", "core"))
    row, col = ("zh", "y"), ("zl", "x", "core")
    return jax.shard_map(
        body,
        mesh=fine,
        in_specs=(
            P(row + col, None),
            P(row + col, None),
            P(row + col, None),
            P(),
            P(row, col, None, None, None),
            P(row, col, None),
            P(row, col),
        ),
        out_specs=(P(col, row, None), P(), P()),
        check_vma=False,
    )
```

```python
import functools
import math

import jax
import jax.numpy as jnp
from jax import lax
from jax.experimental import pallas as pl
from jax.experimental.pallas import tpu as pltpu
from jax.sharding import Mesh, PartitionSpec as P

F32 = jnp.float32
BF16 = jnp.bfloat16
MARK = jax.ShapeDtypeStruct((8, 128), F32)
VMEM_LIMIT = 24 * 1024 * 1024
TILE_LIMIT = 54 * 1024 * 1024


def tile_kernel(pos_ref, live_ref, core_ref, blocks_ref, own_ref, other_ref, out_ref, mark_ref, acc_ref, low_ref, near_ref, rows_ref, sems, near_sems, rows_sems, *, group, n_x):
    n_y, width, _ = out_ref.shape
    blk = blocks_ref.shape[-1]
    tile_cols = acc_ref.shape[0]
    my_core = core_ref[0]
    live = live_ref[0]
    turns = (live + group - 1) // group

    def fetch(turn):
        part = pl.ds(turn * group, group)
        return pltpu.make_async_copy(blocks_ref.at[part], near_ref.at[part], near_sems.at[turn])

    fetch(0).start()
    halves = [pltpu.make_async_copy(r, rows_ref.at[k], rows_sems.at[k]) for k, r in enumerate((own_ref, other_ref))]
    for half in halves:
        half.start()
    lax.fori_loop(1, turns, lambda turn, carry: (fetch(turn).start(), carry)[1], 0)
    acc_ref[...] = jnp.zeros_like(acc_ref)
    for half in halves:
        half.wait()

    def add_group(turn, carry):
        fetch(turn).wait()
        found = []
        for k in range(group):
            slot = turn * group + k
            position = pos_ref[slot]
            source = position // tile_cols
            first = pl.multiple_of(source // (2 * n_x) * blk, blk)
            x_part = (source // 2) % n_x
            rows = rows_ref[(source % 2) ^ my_core, x_part, pl.ds(first, blk), :]
            block = near_ref[slot]
            block = jnp.where(slot < live, block, jnp.zeros_like(block))
            product = lax.dot_general(block, rows, (((0,), (0,)), ((), ())), preferred_element_type=F32)
            found.append((position % tile_cols, product))
        for column, product in found:
            acc_ref[column] += product
        return carry

    lax.fori_loop(0, turns, add_group, 0)
    copies = []
    for y in range(n_y):
        for z in range(width // blk):
            low_ref[y, z * blk : (z + 1) * blk, :] = acc_ref[z * n_y + y].astype(BF16)
        copies.append(pltpu.make_async_copy(low_ref.at[y], out_ref.at[y], sems.at[y]))
        copies[-1].start()
    mark_ref[...] = jnp.zeros_like(mark_ref)
    for copy in copies:
        copy.wait()


def pack_kernel(grad_ref, mask_ref, features_ref, out_ref):
    n_dst, width, n_feat = out_ref.shape
    blk = grad_ref.shape[0]
    n_mine = n_feat // n_dst
    grad_pre = grad_ref[...] * mask_ref[...].astype(BF16)
    for z in range(n_dst):
        out_ref[z, :blk, :] = grad_pre
        for k in range(n_feat // n_mine):
            rows = slice(k * (width - blk), (k + 1) * (width - blk))
            out_ref[z, blk:, k * n_mine : (k + 1) * n_mine] = features_ref[rows, z * n_mine : (z + 1) * n_mine]


def terms_kernel(place_ref, got_ref, keep_ref, send_ref, sum_ref, *, blk):
    n_src, _, n_feat = got_ref.shape
    n_y, n_pair, _ = sum_ref.shape
    n_slice = n_pair // 2
    n_mine = n_y * n_pair
    ones = jnp.ones((8, blk), BF16)
    bias_terms = jnp.zeros((8, n_feat), F32)
    total = jnp.zeros((n_mine, n_feat), F32)
    for s in range(n_src):
        rows = got_ref[s, :blk, :]
        features = [got_ref[s, blk:, k * n_mine : (k + 1) * n_mine] for k in range(n_feat // n_mine)]
        features = jnp.concatenate(features, axis=0)
        total += lax.dot_general(features, rows, (((0,), (0,)), ((), ())), preferred_element_type=F32)
        bias_terms += jnp.dot(ones, rows, preferred_element_type=F32)
    for y in range(n_y):
        sum_ref[y] = total[y * n_pair : (y + 1) * n_pair]
    mine, my_y = place_ref[0], place_ref[1]
    for ref, core in ((keep_ref, mine), (send_ref, 1 - mine)):
        first = pl.multiple_of(core * n_slice, n_slice)
        for y in range(n_y):
            ref[y * n_slice : (y + 1) * n_slice, :] = sum_ref[my_y ^ y, pl.ds(first, n_slice), :]
        ref[n_y * n_slice :, :] = bias_terms


def fold_kernel(in_ref, out_ref, mark_ref):
    mark_ref[...] = jnp.zeros_like(mark_ref)
    total = in_ref[0].astype(F32)
    for s in range(1, in_ref.shape[0]):
        total += in_ref[s].astype(F32)
    out_ref[...] = total.astype(BF16)


def place_kernel(index_ref, *refs, n_slice):
    out_ref = refs[-1]
    offset = 0
    for ref in refs[:-1]:
        for k in range(ref.shape[0] // n_slice):
            first = pl.multiple_of((index_ref[0] ^ index_ref[1 + offset]) * n_slice, n_slice)
            out_ref[pl.ds(first, n_slice), :] = ref[k * n_slice : (k + 1) * n_slice, :].astype(F32)
            offset += 1


def last_kernel(in_ref, weight_ref, rows_ref):
    total = in_ref[0].astype(F32)
    for s in range(1, in_ref.shape[0]):
        total += in_ref[s].astype(F32)
    high = total.astype(BF16)
    low = (total - high.astype(F32)).astype(BF16)
    dims = (((1,), (1,)), ((), ()))
    product = lax.dot_general(high, weight_ref[...], dims, preferred_element_type=F32)
    product += lax.dot_general(low, weight_ref[...], dims, preferred_element_type=F32)
    rows_ref[...] = product.astype(BF16)


def call(kernel, out_shape, scratch=(), n_scalar=0, n_far=0, n_in=1, marked=False, limit=VMEM_LIMIT, out_space=pltpu.VMEM, cost=None):
    smem = pl.BlockSpec(memory_space=pltpu.SMEM)
    vmem = pl.BlockSpec(memory_space=pltpu.VMEM)
    out_specs = jax.tree.map(lambda _: pl.BlockSpec(memory_space=out_space), out_shape)
    if marked:
        out_shape, out_specs = (out_shape, MARK), (out_specs, vmem)
    return pl.pallas_call(
        kernel,
        out_shape=out_shape,
        in_specs=[smem] * n_scalar + [pl.BlockSpec(memory_space=pltpu.HBM)] * n_far + [vmem] * n_in,
        out_specs=out_specs,
        scratch_shapes=list(scratch),
        cost_estimate=cost,
        compiler_params=pltpu.CompilerParams(vmem_limit_bytes=limit),
    )


def swap(value, axis):
    return lax.all_to_all(value, axis, split_axis=0, concat_axis=0, tiled=True)


def trade(value, axis, bit):
    return lax.ppermute(value, axis, [(i, i ^ bit) for i in range(lax.axis_size(axis))])


def body(grad_out, relu_mask, aggregated, weight, adj_blocks, block_pos, block_live):
    blk, n_feat = grad_out.shape
    n_zh, n_y, n_zl, n_x, n_core = (lax.axis_size(a) for a in ("zh", "y", "zl", "x", "core"))
    n_rows = n_zl * blk
    n_pair = n_feat // (n_zl * n_y)
    n_slice = n_pair // n_core
    n_mine = n_feat // n_zl
    sent = call(
        pack_kernel,
        jax.ShapeDtypeStruct((n_zl, blk + blk * n_mine // n_feat, n_feat), BF16),
        n_in=3,
    )(grad_out, relu_mask, aggregated)
    got = swap(sent, "zl")
    core, y_index = (lax.axis_index(a).astype(jnp.int32).reshape(1) for a in ("core", "y"))
    half = jax.ShapeDtypeStruct((n_y * n_slice + 8, n_feat), F32)
    terms, away = call(
        functools.partial(terms_kernel, blk=blk),
        (half, half),
        scratch=[pltpu.VMEM((n_y, n_pair, n_feat), F32)],
        n_scalar=1,
    )(jnp.concatenate([core, y_index]), got)
    rows = got[:, :blk].reshape(n_rows, n_feat)
    own = swap(jnp.broadcast_to(rows, (n_x, n_rows, n_feat)), "x")
    terms = terms + trade(away, "core", 1)
    for bit, n in ((2, 2 * n_slice), (1, n_slice)):
        kept, away, bias = terms[:n], terms[n : 2 * n], terms[2 * n :]
        terms = jnp.concatenate([kept, bias], axis=0) + trade(jnp.concatenate([away, bias], axis=0), "y", bit)
    terms = terms + trade(terms, "zh", 1)
    own, terms = lax.optimization_barrier((own, terms))
    other = lax.ppermute(own, "core", [(0, 1), (1, 0)])
    terms = swap(jnp.broadcast_to(terms, (n_x,) + terms.shape), "x")
    slots = adj_blocks.shape[2]
    group = max(d for d in range(1, 9) if slots % d == 0)
    sent, mark = call(
        functools.partial(tile_kernel, group=group, n_x=n_x),
        jax.ShapeDtypeStruct((n_y, n_zh * blk, n_feat), BF16),
        scratch=[
            pltpu.VMEM((n_zh * n_y, blk, n_feat), F32),
            pltpu.VMEM((n_y, n_zh * blk, n_feat), BF16),
            pltpu.VMEM((slots, blk, blk), BF16),
            pltpu.VMEM((n_core, n_x, n_rows, n_feat), BF16),
            pltpu.SemaphoreType.DMA((n_y,)),
            pltpu.SemaphoreType.DMA((slots // group,)),
            pltpu.SemaphoreType.DMA((n_core,)),
        ],
        n_far=3,
        limit=TILE_LIMIT,
        out_space=pltpu.HBM,
        marked=True,
        cost=pl.CostEstimate(
            flops=2 * slots * blk * blk * n_feat,
            transcendentals=0,
            bytes_accessed=8 * slots * blk * n_feat,
        ),
        n_scalar=3,
        n_in=0,
    )(block_pos.reshape(-1), block_live.reshape(-1), core, adj_blocks[0, 0], own, other)
    terms, sent = lax.optimization_barrier((terms, sent))
    terms = terms.sum(axis=0)
    terms = terms + trade(terms, "zh", 2)
    factor = 1.0 / math.sqrt(blk * n_zh * n_y * n_zl * n_x * n_core)
    terms = terms * factor
    slices = terms[:n_slice].astype(BF16)
    offsets = [0]
    for bit in (1, 2):
        slices = jnp.concatenate([slices, trade(slices, "zl", bit)], axis=0)
        offsets += [o ^ (bit * n_y * n_core) for o in offsets]
    got = swap(sent, "y")
    sent, mark = call(fold_kernel, jax.ShapeDtypeStruct((n_zh * blk, n_feat), BF16), marked=True)(got)
    slices, sent = lax.optimization_barrier((slices, sent))
    pieces = [slices]
    for axis, bit, stride in (("y", 2, n_core), ("y", 1, n_core), ("core", 1, 1)):
        pieces.append(trade(jnp.concatenate(pieces, axis=0), axis, bit))
        offsets += [o ^ (bit * stride) for o in offsets]
    mine = lax.axis_index(("zl", "y", "core")).astype(jnp.int32)
    place = functools.partial(place_kernel, n_slice=n_slice)
    grad_weight = call(place, jax.ShapeDtypeStruct((n_feat, n_feat), F32), n_scalar=1, n_in=len(pieces))(
        jnp.concatenate([mine.reshape(1), jnp.array(offsets, jnp.int32)]), *pieces
    )
    got = swap(sent.reshape(n_zh, blk, n_feat), "zh")
    out_rows = call(last_kernel, jax.ShapeDtypeStruct((blk, n_feat), BF16), n_in=2)(got, weight)
    return out_rows[None], grad_weight, terms[n_slice]


def solution(mesh):
    fine = Mesh(mesh.devices.reshape(4, 4, 4, 4, 2), ("zh", "y", "zl", "x", "core"))
    row, col = ("zh", "y"), ("zl", "x", "core")
    return jax.shard_map(
        body,
        mesh=fine,
        in_specs=(
            P(row + col, None),
            P(row + col, None),
            P(row + col, None),
            P(),
            P(row, col, None, None, None),
            P(row, col, None),
            P(row, col),
        ),
        out_specs=(P(col, row, None), P(), P()),
        check_vma=False,
    )
```

```python
import functools
import math

import jax
import jax.numpy as jnp
from jax import lax
from jax.experimental import pallas as pl
from jax.experimental.pallas import tpu as pltpu
from jax.sharding import Mesh, PartitionSpec as P

F32 = jnp.float32
BF16 = jnp.bfloat16
MARK = jax.ShapeDtypeStruct((8, 128), F32)
VMEM_LIMIT = 24 * 1024 * 1024
TILE_LIMIT = 54 * 1024 * 1024


def tile_kernel(pos_ref, live_ref, core_ref, blocks_ref, own_ref, other_ref, out_ref, mark_ref, acc_ref, low_ref, near_ref, rows_ref, sems, near_sems, rows_sems, *, group, n_x):
    n_y, width, _ = out_ref.shape
    blk = blocks_ref.shape[-1]
    tile_cols = acc_ref.shape[0]
    my_core = core_ref[0]
    live = live_ref[0]
    turns = (live + group - 1) // group

    def fetch(turn):
        part = pl.ds(turn * group, group)
        return pltpu.make_async_copy(blocks_ref.at[part], near_ref.at[part], near_sems.at[turn])

    fetch(0).start()
    halves = [pltpu.make_async_copy(r, rows_ref.at[k], rows_sems.at[k]) for k, r in enumerate((own_ref, other_ref))]
    for half in halves:
        half.start()
    lax.fori_loop(1, turns, lambda turn, carry: (fetch(turn).start(), carry)[1], 0)
    acc_ref[...] = jnp.zeros_like(acc_ref)
    for half in halves:
        half.wait()

    def add_group(turn, carry):
        fetch(turn).wait()
        found = []
        for k in range(group):
            slot = turn * group + k
            position = pos_ref[slot]
            source = position // tile_cols
            first = pl.multiple_of(source // (2 * n_x) * blk, blk)
            x_part = (source // 2) % n_x
            rows = rows_ref[(source % 2) ^ my_core, x_part, pl.ds(first, blk), :]
            block = near_ref[slot]
            block = jnp.where(slot < live, block, jnp.zeros_like(block))
            product = lax.dot_general(block, rows, (((0,), (0,)), ((), ())), preferred_element_type=F32)
            found.append((position % tile_cols, product))
        for column, product in found:
            acc_ref[column] += product
        return carry

    lax.fori_loop(0, turns, add_group, 0)
    copies = []
    for y in range(n_y):
        for z in range(width // blk):
            low_ref[y, z * blk : (z + 1) * blk, :] = acc_ref[z * n_y + y].astype(BF16)
        copies.append(pltpu.make_async_copy(low_ref.at[y], out_ref.at[y], sems.at[y]))
        copies[-1].start()
    mark_ref[...] = jnp.zeros_like(mark_ref)
    for copy in copies:
        copy.wait()


def terms_kernel(place_ref, got_ref, keep_ref, send_ref, sum_ref, *, blk):
    n_src, _, n_feat = got_ref.shape
    n_y, n_pair, _ = sum_ref.shape
    n_slice = n_pair // 2
    n_mine = n_y * n_pair
    ones = jnp.ones((8, blk), BF16)
    bias_terms = jnp.zeros((8, n_feat), F32)
    total = jnp.zeros((n_mine, n_feat), F32)
    for s in range(n_src):
        rows = got_ref[s, :blk, :]
        features = [got_ref[s, blk:, k * n_mine : (k + 1) * n_mine] for k in range(n_feat // n_mine)]
        features = jnp.concatenate(features, axis=0)
        total += lax.dot_general(features, rows, (((0,), (0,)), ((), ())), preferred_element_type=F32)
        bias_terms += jnp.dot(ones, rows, preferred_element_type=F32)
    for y in range(n_y):
        sum_ref[y] = total[y * n_pair : (y + 1) * n_pair]
    mine, my_y = place_ref[0], place_ref[1]
    for ref, core in ((keep_ref, mine), (send_ref, 1 - mine)):
        first = pl.multiple_of(core * n_slice, n_slice)
        for y in range(n_y):
            ref[y * n_slice : (y + 1) * n_slice, :] = sum_ref[my_y ^ y, pl.ds(first, n_slice), :]
        ref[n_y * n_slice :, :] = bias_terms


def fold_kernel(in_ref, out_ref, mark_ref):
    mark_ref[...] = jnp.zeros_like(mark_ref)
    total = in_ref[0].astype(F32)
    for s in range(1, in_ref.shape[0]):
        total += in_ref[s].astype(F32)
    out_ref[...] = total.astype(BF16)


def place_kernel(index_ref, *refs, n_slice):
    out_ref = refs[-1]
    offset = 0
    for ref in refs[:-1]:
        for k in range(ref.shape[0] // n_slice):
            first = pl.multiple_of((index_ref[0] ^ index_ref[1 + offset]) * n_slice, n_slice)
            out_ref[pl.ds(first, n_slice), :] = ref[k * n_slice : (k + 1) * n_slice, :].astype(F32)
            offset += 1


def last_kernel(in_ref, weight_ref, rows_ref):
    total = in_ref[0].astype(F32)
    for s in range(1, in_ref.shape[0]):
        total += in_ref[s].astype(F32)
    high = total.astype(BF16)
    low = (total - high.astype(F32)).astype(BF16)
    dims = (((1,), (1,)), ((), ()))
    product = lax.dot_general(high, weight_ref[...], dims, preferred_element_type=F32)
    product += lax.dot_general(low, weight_ref[...], dims, preferred_element_type=F32)
    rows_ref[...] = product.astype(BF16)


def call(kernel, out_shape, scratch=(), n_scalar=0, n_far=0, n_in=1, marked=False, limit=VMEM_LIMIT, out_space=pltpu.VMEM, cost=None):
    smem = pl.BlockSpec(memory_space=pltpu.SMEM)
    vmem = pl.BlockSpec(memory_space=pltpu.VMEM)
    out_specs = jax.tree.map(lambda _: pl.BlockSpec(memory_space=out_space), out_shape)
    if marked:
        out_shape, out_specs = (out_shape, MARK), (out_specs, vmem)
    return pl.pallas_call(
        kernel,
        out_shape=out_shape,
        in_specs=[smem] * n_scalar + [pl.BlockSpec(memory_space=pltpu.HBM)] * n_far + [vmem] * n_in,
        out_specs=out_specs,
        scratch_shapes=list(scratch),
        cost_estimate=cost,
        compiler_params=pltpu.CompilerParams(vmem_limit_bytes=limit),
    )


def swap(value, axis):
    return lax.all_to_all(value, axis, split_axis=0, concat_axis=0, tiled=True)


def trade(value, axis, bit):
    return lax.ppermute(value, axis, [(i, i ^ bit) for i in range(lax.axis_size(axis))])


def body(grad_out, relu_mask, aggregated, weight, adj_blocks, block_pos, block_live):
    blk, n_feat = grad_out.shape
    n_zh, n_y, n_zl, n_x, n_core = (lax.axis_size(a) for a in ("zh", "y", "zl", "x", "core"))
    n_rows = n_zl * blk
    n_pair = n_feat // (n_zl * n_y)
    n_slice = n_pair // n_core
    n_mine = n_feat // n_zl
    columns = aggregated.reshape(n_feat // n_mine, blk * n_mine // n_feat, n_zl, n_mine).transpose(2, 1, 0, 3)
    columns = columns.reshape(n_zl, blk * n_mine // n_feat, n_feat)
    grad_pre = grad_out * relu_mask.astype(BF16)
    sent = jnp.concatenate([jnp.broadcast_to(grad_pre, (n_zl, blk, n_feat)), columns], axis=1)
    got = swap(sent, "zl")
    core, y_index = (lax.axis_index(a).astype(jnp.int32).reshape(1) for a in ("core", "y"))
    half = jax.ShapeDtypeStruct((n_y * n_slice + 8, n_feat), F32)
    terms, away = call(
        functools.partial(terms_kernel, blk=blk),
        (half, half),
        scratch=[pltpu.VMEM((n_y, n_pair, n_feat), F32)],
        n_scalar=1,
    )(jnp.concatenate([core, y_index]), got)
    rows = got[:, :blk].reshape(n_rows, n_feat)
    own = swap(jnp.broadcast_to(rows, (n_x, n_rows, n_feat)), "x")
    terms = terms + trade(away, "core", 1)
    for bit, n in ((2, 2 * n_slice), (1, n_slice)):
        kept, away, bias = terms[:n], terms[n : 2 * n], terms[2 * n :]
        terms = jnp.concatenate([kept, bias], axis=0) + trade(jnp.concatenate([away, bias], axis=0), "y", bit)
    terms = terms + trade(terms, "zh", 1)
    own, terms = lax.optimization_barrier((own, terms))
    other = lax.ppermute(own, "core", [(0, 1), (1, 0)])
    terms = swap(jnp.broadcast_to(terms, (n_x,) + terms.shape), "x")
    slots = adj_blocks.shape[2]
    group = max(d for d in range(1, 9) if slots % d == 0)
    sent, mark = call(
        functools.partial(tile_kernel, group=group, n_x=n_x),
        jax.ShapeDtypeStruct((n_y, n_zh * blk, n_feat), BF16),
        scratch=[
            pltpu.VMEM((n_zh * n_y, blk, n_feat), F32),
            pltpu.VMEM((n_y, n_zh * blk, n_feat), BF16),
            pltpu.VMEM((slots, blk, blk), BF16),
            pltpu.VMEM((n_core, n_x, n_rows, n_feat), BF16),
            pltpu.SemaphoreType.DMA((n_y,)),
            pltpu.SemaphoreType.DMA((slots // group,)),
            pltpu.SemaphoreType.DMA((n_core,)),
        ],
        n_far=3,
        limit=TILE_LIMIT,
        out_space=pltpu.HBM,
        marked=True,
        cost=pl.CostEstimate(
            flops=2 * slots * blk * blk * n_feat,
            transcendentals=0,
            bytes_accessed=8 * slots * blk * n_feat,
        ),
        n_scalar=3,
        n_in=0,
    )(block_pos.reshape(-1), block_live.reshape(-1), core, adj_blocks[0, 0], own, other)
    terms, sent = lax.optimization_barrier((terms, sent))
    terms = terms.sum(axis=0)
    terms = terms + trade(terms, "zh", 2)
    factor = 1.0 / math.sqrt(blk * n_zh * n_y * n_zl * n_x * n_core)
    terms = terms * factor
    slices = terms[:n_slice].astype(BF16)
    slices = jnp.concatenate([slices] + [trade(slices, "zl", k) for k in range(1, n_zl)], axis=0)
    offsets = [k * n_y * n_core for k in range(n_zl)]
    got = swap(sent, "y")
    sent, mark = call(fold_kernel, jax.ShapeDtypeStruct((n_zh * blk, n_feat), BF16), marked=True)(got)
    slices, sent = lax.optimization_barrier((slices, sent))
    pieces = [slices]
    for axis, bit, stride in (("y", 2, n_core), ("y", 1, n_core), ("core", 1, 1)):
        pieces.append(trade(jnp.concatenate(pieces, axis=0), axis, bit))
        offsets += [o ^ (bit * stride) for o in offsets]
    mine = lax.axis_index(("zl", "y", "core")).astype(jnp.int32)
    place = functools.partial(place_kernel, n_slice=n_slice)
    grad_weight = call(place, jax.ShapeDtypeStruct((n_feat, n_feat), F32), n_scalar=1, n_in=len(pieces))(
        jnp.concatenate([mine.reshape(1), jnp.array(offsets, jnp.int32)]), *pieces
    )
    got = swap(sent.reshape(n_zh, blk, n_feat), "zh")
    out_rows = call(last_kernel, jax.ShapeDtypeStruct((blk, n_feat), BF16), n_in=2)(got, weight)
    return out_rows[None], grad_weight, terms[n_slice]


def solution(mesh):
    fine = Mesh(mesh.devices.reshape(4, 4, 4, 4, 2), ("zh", "y", "zl", "x", "core"))
    row, col = ("zh", "y"), ("zl", "x", "core")
    return jax.shard_map(
        body,
        mesh=fine,
        in_specs=(
            P(row + col, None),
            P(row + col, None),
            P(row + col, None),
            P(),
            P(row, col, None, None, None),
            P(row, col, None),
            P(row, col),
        ),
        out_specs=(P(col, row, None), P(), P()),
        check_vma=False,
    )
```

```python
import functools
import math

import jax
import jax.numpy as jnp
from jax import lax
from jax.experimental import pallas as pl
from jax.experimental.pallas import tpu as pltpu
from jax.sharding import Mesh, PartitionSpec as P

F32 = jnp.float32
BF16 = jnp.bfloat16
MARK = jax.ShapeDtypeStruct((8, 128), F32)
VMEM_LIMIT = 24 * 1024 * 1024
TILE_LIMIT = 54 * 1024 * 1024


def tile_kernel(pos_ref, live_ref, core_ref, blocks_ref, own_ref, other_ref, out_ref, mark_ref, acc_ref, low_ref, near_ref, rows_ref, sems, near_sems, rows_sems, *, group, n_x):
    n_y, width, _ = out_ref.shape
    blk = blocks_ref.shape[-1]
    tile_cols = acc_ref.shape[0]
    my_core = core_ref[0]
    live = live_ref[0]
    turns = (live + group - 1) // group

    def fetch(turn):
        part = pl.ds(turn * group, group)
        return pltpu.make_async_copy(blocks_ref.at[part], near_ref.at[part], near_sems.at[turn])

    fetch(0).start()
    halves = [pltpu.make_async_copy(r, rows_ref.at[k], rows_sems.at[k]) for k, r in enumerate((own_ref, other_ref))]
    for half in halves:
        half.start()
    lax.fori_loop(1, turns, lambda turn, carry: (fetch(turn).start(), carry)[1], 0)
    acc_ref[...] = jnp.zeros_like(acc_ref)
    for half in halves:
        half.wait()

    def add_group(turn, carry):
        fetch(turn).wait()
        found = []
        for k in range(group):
            slot = turn * group + k
            position = pos_ref[slot]
            source = position // tile_cols
            first = pl.multiple_of(source // (2 * n_x) * blk, blk)
            x_part = (source // 2) % n_x
            rows = rows_ref[(source % 2) ^ my_core, x_part, pl.ds(first, blk), :]
            block = near_ref[slot]
            block = jnp.where(slot < live, block, jnp.zeros_like(block))
            product = lax.dot_general(block, rows, (((0,), (0,)), ((), ())), preferred_element_type=F32)
            found.append((position % tile_cols, product))
        for column, product in found:
            acc_ref[column] += product
        return carry

    lax.fori_loop(0, turns, add_group, 0)
    copies = []
    for y in range(n_y):
        for z in range(width // blk):
            low_ref[y, z * blk : (z + 1) * blk, :] = acc_ref[z * n_y + y].astype(BF16)
        copies.append(pltpu.make_async_copy(low_ref.at[y], out_ref.at[y], sems.at[y]))
        copies[-1].start()
    mark_ref[...] = jnp.zeros_like(mark_ref)
    for copy in copies:
        copy.wait()


def terms_kernel(place_ref, got_ref, keep_ref, send_ref, sum_ref, *, blk):
    n_src, _, n_feat = got_ref.shape
    n_y, n_pair, _ = sum_ref.shape
    n_slice = n_pair // 2
    n_mine = n_y * n_pair
    ones = jnp.ones((8, blk), BF16)
    bias_terms = jnp.zeros((8, n_feat), F32)
    total = jnp.zeros((n_mine, n_feat), F32)
    for s in range(n_src):
        rows = got_ref[s, :blk, :]
        features = [got_ref[s, blk:, k * n_mine : (k + 1) * n_mine] for k in range(n_feat // n_mine)]
        features = jnp.concatenate(features, axis=0)
        total += lax.dot_general(features, rows, (((0,), (0,)), ((), ())), preferred_element_type=F32)
        bias_terms += jnp.dot(ones, rows, preferred_element_type=F32)
    for y in range(n_y):
        sum_ref[y] = total[y * n_pair : (y + 1) * n_pair]
    mine, my_y = place_ref[0], place_ref[1]
    for ref, core in ((keep_ref, mine), (send_ref, 1 - mine)):
        first = pl.multiple_of(core * n_slice, n_slice)
        for y in range(n_y):
            ref[y * n_slice : (y + 1) * n_slice, :] = sum_ref[my_y ^ y, pl.ds(first, n_slice), :]
        ref[n_y * n_slice :, :] = bias_terms


def fold_kernel(in_ref, out_ref, mark_ref):
    mark_ref[...] = jnp.zeros_like(mark_ref)
    total = in_ref[0].astype(F32)
    for s in range(1, in_ref.shape[0]):
        total += in_ref[s].astype(F32)
    out_ref[...] = total.astype(BF16)


def place_kernel(index_ref, *refs, n_slice):
    out_ref = refs[-1]
    offset = 0
    for ref in refs[:-1]:
        for k in range(ref.shape[0] // n_slice):
            first = pl.multiple_of((index_ref[0] ^ index_ref[1 + offset]) * n_slice, n_slice)
            out_ref[pl.ds(first, n_slice), :] = ref[k * n_slice : (k + 1) * n_slice, :].astype(F32)
            offset += 1


def last_kernel(in_ref, weight_ref, rows_ref):
    total = in_ref[0].astype(F32)
    for s in range(1, in_ref.shape[0]):
        total += in_ref[s].astype(F32)
    high = total.astype(BF16)
    low = (total - high.astype(F32)).astype(BF16)
    dims = (((1,), (1,)), ((), ()))
    product = lax.dot_general(high, weight_ref[...], dims, preferred_element_type=F32)
    product += lax.dot_general(low, weight_ref[...], dims, preferred_element_type=F32)
    rows_ref[...] = product.astype(BF16)


def call(kernel, out_shape, scratch=(), n_scalar=0, n_far=0, n_in=1, marked=False, limit=VMEM_LIMIT, out_space=pltpu.VMEM, cost=None):
    smem = pl.BlockSpec(memory_space=pltpu.SMEM)
    vmem = pl.BlockSpec(memory_space=pltpu.VMEM)
    out_specs = jax.tree.map(lambda _: pl.BlockSpec(memory_space=out_space), out_shape)
    if marked:
        out_shape, out_specs = (out_shape, MARK), (out_specs, vmem)
    return pl.pallas_call(
        kernel,
        out_shape=out_shape,
        in_specs=[smem] * n_scalar + [pl.BlockSpec(memory_space=pltpu.HBM)] * n_far + [vmem] * n_in,
        out_specs=out_specs,
        scratch_shapes=list(scratch),
        cost_estimate=cost,
        compiler_params=pltpu.CompilerParams(vmem_limit_bytes=limit),
    )


def swap(value, axis):
    return lax.all_to_all(value, axis, split_axis=0, concat_axis=0, tiled=True)


def trade(value, axis, bit):
    return lax.ppermute(value, axis, [(i, i ^ bit) for i in range(lax.axis_size(axis))])


def body(grad_out, relu_mask, aggregated, weight, adj_blocks, block_pos, block_live):
    blk, n_feat = grad_out.shape
    n_zh, n_y, n_zl, n_x, n_core = (lax.axis_size(a) for a in ("zh", "y", "zl", "x", "core"))
    n_rows = n_zl * blk
    n_pair = n_feat // (n_zl * n_y)
    n_slice = n_pair // n_core
    n_mine = n_feat // n_zl
    columns = aggregated.reshape(n_feat // n_mine, blk * n_mine // n_feat, n_zl, n_mine).transpose(2, 1, 0, 3)
    columns = columns.reshape(n_zl, blk * n_mine // n_feat, n_feat)
    grad_pre = grad_out * relu_mask.astype(BF16)
    sent = jnp.concatenate([jnp.broadcast_to(grad_pre, (n_zl, blk, n_feat)), columns], axis=1)
    got = swap(sent, "zl")
    core, y_index = (lax.axis_index(a).astype(jnp.int32).reshape(1) for a in ("core", "y"))
    half = jax.ShapeDtypeStruct((n_y * n_slice + 8, n_feat), F32)
    terms, away = call(
        functools.partial(terms_kernel, blk=blk),
        (half, half),
        scratch=[pltpu.VMEM((n_y, n_pair, n_feat), F32)],
        n_scalar=1,
    )(jnp.concatenate([core, y_index]), got)
    rows = got[:, :blk].reshape(n_rows, n_feat)
    own = swap(jnp.broadcast_to(rows, (n_x, n_rows, n_feat)), "x")
    terms = terms + trade(away, "core", 1)
    for bit, n in ((2, 2 * n_slice), (1, n_slice)):
        kept, away, bias = terms[:n], terms[n : 2 * n], terms[2 * n :]
        terms = jnp.concatenate([kept, bias], axis=0) + trade(jnp.concatenate([away, bias], axis=0), "y", bit)
    own, terms = lax.optimization_barrier((own, terms))
    other = lax.ppermute(own, "core", [(0, 1), (1, 0)])
    terms = swap(jnp.broadcast_to(terms, (n_zh,) + terms.shape), "zh")
    slots = adj_blocks.shape[2]
    group = max(d for d in range(1, 9) if slots % d == 0)
    sent, mark = call(
        functools.partial(tile_kernel, group=group, n_x=n_x),
        jax.ShapeDtypeStruct((n_y, n_zh * blk, n_feat), BF16),
        scratch=[
            pltpu.VMEM((n_zh * n_y, blk, n_feat), F32),
            pltpu.VMEM((n_y, n_zh * blk, n_feat), BF16),
            pltpu.VMEM((slots, blk, blk), BF16),
            pltpu.VMEM((n_core, n_x, n_rows, n_feat), BF16),
            pltpu.SemaphoreType.DMA((n_y,)),
            pltpu.SemaphoreType.DMA((slots // group,)),
            pltpu.SemaphoreType.DMA((n_core,)),
        ],
        n_far=3,
        limit=TILE_LIMIT,
        out_space=pltpu.HBM,
        marked=True,
        cost=pl.CostEstimate(
            flops=2 * slots * blk * blk * n_feat,
            transcendentals=0,
            bytes_accessed=8 * slots * blk * n_feat,
        ),
        n_scalar=3,
        n_in=0,
    )(block_pos.reshape(-1), block_live.reshape(-1), core, adj_blocks[0, 0], own, other)
    terms, sent = lax.optimization_barrier((terms, sent))
    terms = terms.sum(axis=0)
    for bit in (1, 2):
        terms = terms + trade(terms, "x", bit)
    factor = 1.0 / math.sqrt(blk * n_zh * n_y * n_zl * n_x * n_core)
    terms = terms * factor
    slices = terms[:n_slice].astype(BF16)
    offsets = [0]
    for bit in (1, 2):
        slices = jnp.concatenate([slices, trade(slices, "zl", bit)], axis=0)
        offsets += [o ^ (bit * n_y * n_core) for o in offsets]
    got = swap(sent, "y")
    sent, mark = call(fold_kernel, jax.ShapeDtypeStruct((n_zh * blk, n_feat), BF16), marked=True)(got)
    slices, sent = lax.optimization_barrier((slices, sent))
    pieces = [slices]
    for axis, bit, stride in (("y", 2, n_core), ("y", 1, n_core), ("core", 1, 1)):
        pieces.append(trade(jnp.concatenate(pieces, axis=0), axis, bit))
        offsets += [o ^ (bit * stride) for o in offsets]
    mine = lax.axis_index(("zl", "y", "core")).astype(jnp.int32)
    place = functools.partial(place_kernel, n_slice=n_slice)
    grad_weight = call(place, jax.ShapeDtypeStruct((n_feat, n_feat), F32), n_scalar=1, n_in=len(pieces))(
        jnp.concatenate([mine.reshape(1), jnp.array(offsets, jnp.int32)]), *pieces
    )
    got = swap(sent.reshape(n_zh, blk, n_feat), "zh")
    out_rows = call(last_kernel, jax.ShapeDtypeStruct((blk, n_feat), BF16), n_in=2)(got, weight)
    return out_rows[None], grad_weight, terms[n_slice]


def solution(mesh):
    fine = Mesh(mesh.devices.reshape(4, 4, 4, 4, 2), ("zh", "y", "zl", "x", "core"))
    row, col = ("zh", "y"), ("zl", "x", "core")
    return jax.shard_map(
        body,
        mesh=fine,
        in_specs=(
            P(row + col, None),
            P(row + col, None),
            P(row + col, None),
            P(),
            P(row, col, None, None, None),
            P(row, col, None),
            P(row, col),
        ),
        out_specs=(P(col, row, None), P(), P()),
        check_vma=False,
    )
```

```python
import functools
import math

import jax
import jax.numpy as jnp
from jax import lax
from jax.experimental import pallas as pl
from jax.experimental.pallas import tpu as pltpu
from jax.sharding import Mesh, PartitionSpec as P

F32 = jnp.float32
BF16 = jnp.bfloat16
MARK = jax.ShapeDtypeStruct((8, 128), F32)
VMEM_LIMIT = 24 * 1024 * 1024
TILE_LIMIT = 54 * 1024 * 1024


def tile_kernel(pos_ref, live_ref, core_ref, blocks_ref, own_ref, other_ref, out_ref, mark_ref, acc_ref, low_ref, near_ref, rows_ref, sems, near_sems, rows_sems, *, group, n_x):
    n_y, width, _ = out_ref.shape
    blk = blocks_ref.shape[-1]
    tile_cols = acc_ref.shape[0]
    my_core = core_ref[0]
    live = live_ref[0]
    turns = (live + group - 1) // group

    def fetch(turn):
        part = pl.ds(turn * group, group)
        return pltpu.make_async_copy(blocks_ref.at[part], near_ref.at[part], near_sems.at[turn])

    fetch(0).start()
    halves = [pltpu.make_async_copy(r, rows_ref.at[k], rows_sems.at[k]) for k, r in enumerate((own_ref, other_ref))]
    for half in halves:
        half.start()
    lax.fori_loop(1, turns, lambda turn, carry: (fetch(turn).start(), carry)[1], 0)
    acc_ref[...] = jnp.zeros_like(acc_ref)
    for half in halves:
        half.wait()

    def add_group(turn, carry):
        fetch(turn).wait()
        found = []
        for k in range(group):
            slot = turn * group + k
            position = pos_ref[slot]
            source = position // tile_cols
            first = pl.multiple_of(source // (2 * n_x) * blk, blk)
            x_part = (source // 2) % n_x
            rows = rows_ref[(source % 2) ^ my_core, x_part, pl.ds(first, blk), :]
            block = near_ref[slot]
            block = jnp.where(slot < live, block, jnp.zeros_like(block))
            product = lax.dot_general(block, rows, (((0,), (0,)), ((), ())), preferred_element_type=F32)
            found.append((position % tile_cols, product))
        for column, product in found:
            acc_ref[column] += product
        return carry

    lax.fori_loop(0, turns, add_group, 0)
    copies = []
    for y in range(n_y):
        for z in range(width // blk):
            low_ref[y, z * blk : (z + 1) * blk, :] = acc_ref[z * n_y + y].astype(BF16)
        copies.append(pltpu.make_async_copy(low_ref.at[y], out_ref.at[y], sems.at[y]))
        copies[-1].start()
    mark_ref[...] = jnp.zeros_like(mark_ref)
    for copy in copies:
        copy.wait()


def terms_kernel(place_ref, got_ref, keep_ref, send_ref, sum_ref, *, blk):
    n_src, _, n_feat = got_ref.shape
    n_y, n_pair, _ = sum_ref.shape
    n_slice = n_pair // 2
    n_mine = n_y * n_pair
    ones = jnp.ones((8, blk), BF16)
    bias_terms = jnp.zeros((8, n_feat), F32)
    total = jnp.zeros((n_mine, n_feat), F32)
    for s in range(n_src):
        rows = got_ref[s, :blk, :]
        features = [got_ref[s, blk:, k * n_mine : (k + 1) * n_mine] for k in range(n_feat // n_mine)]
        features = jnp.concatenate(features, axis=0)
        total += lax.dot_general(features, rows, (((0,), (0,)), ((), ())), preferred_element_type=F32)
        bias_terms += jnp.dot(ones, rows, preferred_element_type=F32)
    for y in range(n_y):
        sum_ref[y] = total[y * n_pair : (y + 1) * n_pair]
    mine, my_y = place_ref[0], place_ref[1]
    for ref, core in ((keep_ref, mine), (send_ref, 1 - mine)):
        first = pl.multiple_of(core * n_slice, n_slice)
        for y in range(n_y):
            ref[y * n_slice : (y + 1) * n_slice, :] = sum_ref[my_y ^ y, pl.ds(first, n_slice), :]
        ref[n_y * n_slice :, :] = bias_terms


def fold_kernel(in_ref, out_ref, mark_ref):
    mark_ref[...] = jnp.zeros_like(mark_ref)
    total = in_ref[0].astype(F32)
    for s in range(1, in_ref.shape[0]):
        total += in_ref[s].astype(F32)
    out_ref[...] = total.astype(BF16)


def place_kernel(index_ref, *refs, n_slice):
    out_ref = refs[-1]
    offset = 0
    for ref in refs[:-1]:
        for k in range(ref.shape[0] // n_slice):
            first = pl.multiple_of((index_ref[0] ^ index_ref[1 + offset]) * n_slice, n_slice)
            out_ref[pl.ds(first, n_slice), :] = ref[k * n_slice : (k + 1) * n_slice, :].astype(F32)
            offset += 1


def last_kernel(in_ref, weight_ref, rows_ref):
    total = in_ref[0].astype(F32)
    for s in range(1, in_ref.shape[0]):
        total += in_ref[s].astype(F32)
    high = total.astype(BF16)
    low = (total - high.astype(F32)).astype(BF16)
    dims = (((1,), (1,)), ((), ()))
    product = lax.dot_general(high, weight_ref[...], dims, preferred_element_type=F32)
    product += lax.dot_general(low, weight_ref[...], dims, preferred_element_type=F32)
    rows_ref[...] = product.astype(BF16)


def call(kernel, out_shape, scratch=(), n_scalar=0, n_far=0, n_in=1, marked=False, limit=VMEM_LIMIT, out_space=pltpu.VMEM, cost=None):
    smem = pl.BlockSpec(memory_space=pltpu.SMEM)
    vmem = pl.BlockSpec(memory_space=pltpu.VMEM)
    out_specs = jax.tree.map(lambda _: pl.BlockSpec(memory_space=out_space), out_shape)
    if marked:
        out_shape, out_specs = (out_shape, MARK), (out_specs, vmem)
    return pl.pallas_call(
        kernel,
        out_shape=out_shape,
        in_specs=[smem] * n_scalar + [pl.BlockSpec(memory_space=pltpu.HBM)] * n_far + [vmem] * n_in,
        out_specs=out_specs,
        scratch_shapes=list(scratch),
        cost_estimate=cost,
        compiler_params=pltpu.CompilerParams(vmem_limit_bytes=limit),
    )


def swap(value, axis):
    return lax.all_to_all(value, axis, split_axis=0, concat_axis=0, tiled=True)


def trade(value, axis, bit):
    return lax.ppermute(value, axis, [(i, i ^ bit) for i in range(lax.axis_size(axis))])


def body(grad_out, relu_mask, aggregated, weight, adj_blocks, block_pos, block_live):
    blk, n_feat = grad_out.shape
    n_zh, n_y, n_zl, n_x, n_core = (lax.axis_size(a) for a in ("zh", "y", "zl", "x", "core"))
    n_rows = n_zl * blk
    n_pair = n_feat // (n_zl * n_y)
    n_slice = n_pair // n_core
    n_mine = n_feat // n_zl
    columns = aggregated.reshape(n_feat // n_mine, blk * n_mine // n_feat, n_zl, n_mine).transpose(2, 1, 0, 3)
    columns = columns.reshape(n_zl, blk * n_mine // n_feat, n_feat)
    grad_pre = grad_out * relu_mask.astype(BF16)
    sent = jnp.concatenate([jnp.broadcast_to(grad_pre, (n_zl, blk, n_feat)), columns], axis=1)
    got = swap(sent, "zl")
    core, y_index = (lax.axis_index(a).astype(jnp.int32).reshape(1) for a in ("core", "y"))
    half = jax.ShapeDtypeStruct((n_y * n_slice + 8, n_feat), F32)
    terms, away = call(
        functools.partial(terms_kernel, blk=blk),
        (half, half),
        scratch=[pltpu.VMEM((n_y, n_pair, n_feat), F32)],
        n_scalar=1,
    )(jnp.concatenate([core, y_index]), got)
    rows = got[:, :blk].reshape(n_rows, n_feat)
    own = swap(jnp.broadcast_to(rows, (n_x, n_rows, n_feat)), "x")
    terms = terms + trade(away, "core", 1)
    for bit, n in ((2, 2 * n_slice), (1, n_slice)):
        kept, away, bias = terms[:n], terms[n : 2 * n], terms[2 * n :]
        terms = jnp.concatenate([kept, bias], axis=0) + trade(jnp.concatenate([away, bias], axis=0), "y", bit)
    own, terms = lax.optimization_barrier((own, terms))
    other = lax.ppermute(own, "core", [(0, 1), (1, 0)])
    terms = swap(jnp.broadcast_to(terms, (n_zh,) + terms.shape), "zh")
    slots = adj_blocks.shape[2]
    group = max(d for d in range(1, 18) if slots % d == 0)
    sent, mark = call(
        functools.partial(tile_kernel, group=group, n_x=n_x),
        jax.ShapeDtypeStruct((n_y, n_zh * blk, n_feat), BF16),
        scratch=[
            pltpu.VMEM((n_zh * n_y, blk, n_feat), F32),
            pltpu.VMEM((n_y, n_zh * blk, n_feat), BF16),
            pltpu.VMEM((slots, blk, blk), BF16),
            pltpu.VMEM((n_core, n_x, n_rows, n_feat), BF16),
            pltpu.SemaphoreType.DMA((n_y,)),
            pltpu.SemaphoreType.DMA((slots // group,)),
            pltpu.SemaphoreType.DMA((n_core,)),
        ],
        n_far=3,
        limit=TILE_LIMIT,
        out_space=pltpu.HBM,
        marked=True,
        cost=pl.CostEstimate(
            flops=2 * slots * blk * blk * n_feat,
            transcendentals=0,
            bytes_accessed=8 * slots * blk * n_feat,
        ),
        n_scalar=3,
        n_in=0,
    )(block_pos.reshape(-1), block_live.reshape(-1), core, adj_blocks[0, 0], own, other)
    terms, sent = lax.optimization_barrier((terms, sent))
    terms = terms.sum(axis=0)
    for bit in (1, 2):
        terms = terms + trade(terms, "x", bit)
    factor = 1.0 / math.sqrt(blk * n_zh * n_y * n_zl * n_x * n_core)
    terms = terms * factor
    slices = terms[:n_slice].astype(BF16)
    offsets = [0]
    for bit in (1, 2):
        slices = jnp.concatenate([slices, trade(slices, "zl", bit)], axis=0)
        offsets += [o ^ (bit * n_y * n_core) for o in offsets]
    got = swap(sent, "y")
    sent, mark = call(fold_kernel, jax.ShapeDtypeStruct((n_zh * blk, n_feat), BF16), marked=True)(got)
    slices, sent = lax.optimization_barrier((slices, sent))
    pieces = [slices]
    for axis, bit, stride in (("y", 2, n_core), ("y", 1, n_core), ("core", 1, 1)):
        pieces.append(trade(jnp.concatenate(pieces, axis=0), axis, bit))
        offsets += [o ^ (bit * stride) for o in offsets]
    mine = lax.axis_index(("zl", "y", "core")).astype(jnp.int32)
    place = functools.partial(place_kernel, n_slice=n_slice)
    grad_weight = call(place, jax.ShapeDtypeStruct((n_feat, n_feat), F32), n_scalar=1, n_in=len(pieces))(
        jnp.concatenate([mine.reshape(1), jnp.array(offsets, jnp.int32)]), *pieces
    )
    got = swap(sent.reshape(n_zh, blk, n_feat), "zh")
    out_rows = call(last_kernel, jax.ShapeDtypeStruct((blk, n_feat), BF16), n_in=2)(got, weight)
    return out_rows[None], grad_weight, terms[n_slice]


def solution(mesh):
    fine = Mesh(mesh.devices.reshape(4, 4, 4, 4, 2), ("zh", "y", "zl", "x", "core"))
    row, col = ("zh", "y"), ("zl", "x", "core")
    return jax.shard_map(
        body,
        mesh=fine,
        in_specs=(
            P(row + col, None),
            P(row + col, None),
            P(row + col, None),
            P(),
            P(row, col, None, None, None),
            P(row, col, None),
            P(row, col),
        ),
        out_specs=(P(col, row, None), P(), P()),
        check_vma=False,
    )
```
